32 devices in a mesh: dp: 8 (over z, x), tensor: 4 (over y, core).
Axes of the slice: x: 2, y: 2, z: 4, core: 2. Of those that a mesh axis runs over, the one named last changes fastest.
Arguments:
- hidden_in: bfloat16 [4096, 3072], P(('dp', 'tensor')), may hold values from -6 to 6
- cotangent: float32 [4096, 3072], P(('dp', 'tensor')), may hold values from -6 to 6
- lengths: int32 [8], P('dp'), may hold values from 256 to 512, as said below
- gain_attn: bfloat16 [3072], P('dp'), may hold values from 0.5 to 1.5
- w_qkv: bfloat16 [3, 3072, 3072], P(None, 'dp', 'tensor'), may hold values from -0.109375 to 0.109375
- w_out: bfloat16 [3072, 3072], P('tensor', 'dp'), may hold values from -1 to 1
- gain_mlp: bfloat16 [3072], P('dp'), may hold values from 0.5 to 1.5
- w_gate_up: bfloat16 [3072, 2, 8192], P('dp', None, 'tensor'), may hold values from -0.109375 to 0.109375
- w_down: bfloat16 [8192, 3072], P('tensor', 'dp'), may hold values from -0.0625 to 0.0625
Outputs:
- layer_out: float32 [4096, 3072], P(('dp', 'tensor'))
- grad_in: float32 [4096, 3072], P(('dp', 'tensor'))
- grad_gain_attn: float32 [3072], P('dp')
- grad_qkv: float32 [3, 3072, 3072], P(None, 'dp', 'tensor')
- grad_out: float32 [3072, 3072], P('tensor', 'dp')
- grad_gain_mlp: float32 [3072], P('dp')
- grad_gate_up: float32 [3072, 2, 8192], P('dp', None, 'tensor')
- grad_down: float32 [8192, 3072], P('tensor', 'dp')
The draws below stay inside these ranges and needn't reach their ends.
Inputs may be any that keep to these rules, and one draw needn't show every extreme that they name: Group g holds one sequence in its first lengths[g] rows; its other rows are padding. Some group is full and some group holds exactly 256 live rows.
All inputs are finite; a program needn't handle non-finite values.
Results may differ from the reference program's by a relative error of at most 0.019.
Values may be sent and summed in bfloat16 or wider, within the bound.
No kernel may reach another device: no remote copies, remote signals or barrier semaphores. Data moves between devices by JAX's collectives and lax.ppermute only.
A program may use at most 256 MiB of HBM per device.

```python
import math
import jax
import jax.numpy as jnp
from jax import lax

D = 3072
HEAD_DIM = 96
FF = 8192
GRP = 512
SHORTEST = 256
GROUPS = 8
TOKENS = 4096


def draw_lengths(key, part):
    first_key, second_key = jax.random.split(key)
    length_draw = jax.random.randint(first_key, (GROUPS,), SHORTEST, GRP + 1, dtype=jnp.int32)
    group_order = jax.random.permutation(second_key, GROUPS)
    length_draw = length_draw.at[group_order[0]].set(GRP)
    return length_draw.at[group_order[1]].set(SHORTEST)


def block_scale(stream_key, extent, shards, smallest, largest):
    level = 1.0
    for dim, parts in shards:
        draws = jax.random.uniform(jax.random.fold_in(jax.random.fold_in(stream_key, 6), dim), (parts,), jnp.float32, smallest / len(shards), largest / len(shards))
        level = level * jnp.repeat(jnp.exp(draws), extent[dim] // parts).reshape((-1,) + (1,) * (len(extent) - 1 - dim))
    return level


def gaussian(own_key, dims, spread, limit, pieces=(), kind=jnp.bfloat16):
    entries = spread * jax.random.normal(own_key, dims, jnp.float32)
    if pieces:
        entries = entries * block_scale(own_key, dims, pieces, -0.22, 0.18)
    return jnp.clip(entries, -limit, limit).astype(kind)


def setup_inputs(seed: int = 0) -> dict:
    streams_of = jax.random.split(jax.random.key(seed), 10)
    return {
        "hidden_in": gaussian(streams_of[0], (TOKENS, D), 1.0, 6.0, ((0, 32),)),
        "cotangent": gaussian(streams_of[1], (TOKENS, D), 1.0, 6.0, ((0, 32),), jnp.float32),
        "lengths": draw_lengths(jax.random.fold_in(streams_of[9], 71), 0),
        "gain_attn": jnp.clip(1.0 + 0.1 * jax.random.normal(streams_of[3], (D,), jnp.float32), 0.5, 1.5).astype(jnp.bfloat16),
        "w_qkv": gaussian(streams_of[4], (3, D, D), D ** -0.5, 0.109375, ((1, 8), (2, 4))),
        "w_out": gaussian(streams_of[5], (D, D), (max(5 * D // GRP, 1)) ** -0.5, 1.0, ((0, 4), (1, 8))),
        "gain_mlp": jnp.clip(1.0 + 0.1 * jax.random.normal(streams_of[6], (D,), jnp.float32), 0.5, 1.5).astype(jnp.bfloat16),
        "w_gate_up": gaussian(streams_of[7], (D, 2, FF), D ** -0.5, 0.109375, ((0, 8), (2, 4))),
        "w_down": gaussian(streams_of[8], (FF, D), FF ** -0.5, 0.0625, ((0, 4), (1, 8))),
    }


NORM_EPS = 1e-05
ROPE_BASE = 10000.0

def rope_tables(row_count, head_width):
    positions = jnp.arange(row_count).astype(jnp.float32)
    exponent = jnp.arange(head_width // 2).astype(jnp.float32) * (2.0 / head_width)
    frequency = ROPE_BASE ** (-exponent)
    angles = positions[:, None] * frequency[None, :]
    cosine = jnp.concatenate([jnp.cos(angles), jnp.cos(angles)], axis=1)[:, None, :]
    sine_table = jnp.concatenate([jnp.sin(angles), jnp.sin(angles)], axis=1)[:, None, :]
    return (cosine, sine_table)

def rotate(values):
    half_width = values.shape[-1] // 2
    return jnp.concatenate([-values[..., half_width:], values[..., :half_width]], axis=-1)

def rotate_back(values):
    half_width = values.shape[-1] // 2
    return jnp.concatenate([values[..., half_width:], -values[..., :half_width]], axis=-1)

def rms_unit(values):
    scale_inv = lax.rsqrt(lax.optimization_barrier(jnp.mean(values * values, axis=1, keepdims=True)) + NORM_EPS)
    return (values * scale_inv, scale_inv)

def norm_back(grad_normed, gain, unit, scale_inv):
    grad_unit = grad_normed * gain
    return scale_inv * (grad_unit - unit * lax.optimization_barrier(jnp.mean(grad_unit * unit, axis=1, keepdims=True)))

def mix(form, left, right):
    return jnp.einsum(form, left.astype(jnp.float32), right.astype(jnp.float32))

def score_block(queries, keys_all, offset, length, block_rows):
    row_count = keys_all.shape[0]
    key_ids = jnp.arange(row_count, dtype=jnp.int32)
    row_ids = offset + jnp.arange(block_rows, dtype=jnp.int32)
    allowed = (key_ids[None, :] <= row_ids[:, None]) & ((row_ids[:, None] < length) == (key_ids[None, :] < length))
    query_block = lax.dynamic_slice_in_dim(queries, offset, block_rows, 0)
    scores = mix('qhd,khd->hqk', query_block, keys_all) * (1.0 / math.sqrt(queries.shape[2]))
    return (jnp.where(allowed[None], scores, -jnp.inf), query_block)

def block_offsets(row_count, block_rows):
    return (jnp.arange(row_count // block_rows) * block_rows).astype(jnp.int32)

def attend(queries, keys_all, values, length, block_rows):
    row_count, head_count, head_width = queries.shape

    def one_block(offset):
        scores, query_block = score_block(queries, keys_all, offset, length, block_rows)
        row_max = lax.optimization_barrier(jnp.max(scores, axis=2, keepdims=True))
        log_total = row_max + jnp.log(lax.optimization_barrier(jnp.sum(jnp.exp(scores - row_max), axis=2, keepdims=True)))
        attn_prob = jnp.exp(scores - log_total).astype(jnp.bfloat16)
        mixed = mix('hqk,khd->qhd', attn_prob, values).astype(jnp.bfloat16)
        return (mixed, log_total[..., 0])
    mixed, log_total = lax.map(one_block, block_offsets(row_count, block_rows))
    mixed = mixed.reshape(row_count, head_count, head_width)
    log_total = jnp.transpose(log_total, (1, 0, 2)).reshape(head_count, row_count)
    return (mixed, log_total)

def attend_back(queries, keys_all, values, mixed, log_total, grad_mixed, length, block_rows):
    row_count, head_count, head_width = queries.shape
    delta_all = lax.optimization_barrier(jnp.sum(grad_mixed.astype(jnp.float32) * mixed.astype(jnp.float32), axis=2))

    def one_block(totals, offset):
        grad_keys, grad_values = totals
        scores, query_block = score_block(queries, keys_all, offset, length, block_rows)
        log_block = lax.dynamic_slice_in_dim(log_total, offset, block_rows, 1)
        prob_full = jnp.exp(scores - log_block[..., None])
        prob_half = prob_full.astype(jnp.bfloat16)
        grad_block = lax.dynamic_slice_in_dim(grad_mixed, offset, block_rows, 0)
        delta_block = lax.dynamic_slice_in_dim(delta_all, offset, block_rows, 0)
        grad_prob = mix('qhd,khd->hqk', grad_block, values)
        grad_score = (prob_full * (grad_prob - jnp.transpose(delta_block)[..., None]) * (1.0 / math.sqrt(head_width))).astype(jnp.bfloat16)
        grad_query = mix('hqk,khd->qhd', grad_score, keys_all)
        grad_keys = grad_keys + mix('hqk,qhd->khd', grad_score, query_block)
        grad_values = grad_values + mix('hqk,qhd->khd', prob_half, grad_block)
        return ((grad_keys, grad_values), grad_query)
    zeros = jnp.zeros((row_count, head_count, head_width), jnp.float32)
    (grad_keys, grad_values), grad_query = lax.scan(one_block, (zeros, zeros), block_offsets(row_count, block_rows))
    return (grad_query.reshape(row_count, head_count, head_width), grad_keys, grad_values)

def layer_group(inputs, cot_rows, length, gain_attn, w_qkv, w_out, gain_mlp, w_gate_up, w_down):
    row_count = inputs.shape[0]
    block_rows = min(512, row_count)
    head_count = w_qkv.shape[2] // HEAD_DIM
    shape_heads = (row_count, head_count, HEAD_DIM)
    row_ids = jnp.arange(row_count, dtype=jnp.int32)
    live = (row_ids < length).astype(jnp.float32)[:, None]
    cosine, sine_table = rope_tables(row_count, HEAD_DIM)
    input_f = inputs.astype(jnp.float32)
    unit_first, scale_first = rms_unit(input_f)
    normed_first = (unit_first * gain_attn.astype(jnp.float32)).astype(jnp.bfloat16)
    projected = mix('td,jde->jte', normed_first, w_qkv)
    query_raw = projected[0].reshape(shape_heads)
    key_raw = projected[1].reshape(shape_heads)
    queries = (query_raw * cosine + rotate(query_raw) * sine_table).astype(jnp.bfloat16)
    keys_rot = (key_raw * cosine + rotate(key_raw) * sine_table).astype(jnp.bfloat16)
    values = projected[2].reshape(shape_heads).astype(jnp.bfloat16)
    mixed, log_total = attend(queries, keys_rot, values, length, block_rows)
    attn_flat = mixed.reshape(row_count, -1)
    middle = input_f + jnp.dot(attn_flat, w_out, preferred_element_type=jnp.float32)
    unit_second, scale_second = rms_unit(middle)
    normed_second = (unit_second * gain_mlp.astype(jnp.float32)).astype(jnp.bfloat16)
    gate_up = mix('td,djf->jtf', normed_second, w_gate_up)
    gate_part = gate_up[0]
    up_part = gate_up[1]
    sigmoid_gate = jax.nn.sigmoid(gate_part)
    activated = (gate_part * sigmoid_gate * up_part).astype(jnp.bfloat16)
    result = (middle + jnp.dot(activated, w_down, preferred_element_type=jnp.float32)) * live
    grad_rows = cot_rows * live
    grad_half = grad_rows.astype(jnp.bfloat16)
    grad_down = jnp.dot(activated.T, grad_half, preferred_element_type=jnp.float32)
    grad_act = jnp.dot(grad_half, w_down.T, preferred_element_type=jnp.float32)
    grad_gu = jnp.stack([grad_act * up_part * sigmoid_gate * (1.0 + gate_part * (1.0 - sigmoid_gate)), grad_act * gate_part * sigmoid_gate]).astype(jnp.bfloat16)
    grad_gate_up = mix('td,jtf->djf', normed_second, grad_gu)
    grad_second = mix('jtf,djf->td', grad_gu, w_gate_up)
    grad_gain_mlp = lax.optimization_barrier(jnp.sum(grad_second * unit_second, axis=0))
    grad_middle = grad_rows + norm_back(grad_second, gain_mlp.astype(jnp.float32), unit_second, scale_second)
    middle_half = grad_middle.astype(jnp.bfloat16)
    grad_out = jnp.dot(attn_flat.T, middle_half, preferred_element_type=jnp.float32)
    grad_mixed = jnp.dot(middle_half, w_out.T, preferred_element_type=jnp.float32).astype(jnp.bfloat16).reshape(shape_heads)
    grad_query, grad_keys, grad_values = attend_back(queries, keys_rot, values, mixed, log_total, grad_mixed, length, block_rows)
    query_back = grad_query * cosine + rotate_back(grad_query * sine_table)
    key_back = grad_keys * cosine + rotate_back(grad_keys * sine_table)
    grad_proj = jnp.stack([query_back, key_back, grad_values]).astype(jnp.bfloat16).reshape(3, row_count, -1)
    grad_qkv = mix('td,jte->jde', normed_first, grad_proj)
    grad_first = mix('jte,jde->td', grad_proj, w_qkv)
    grad_gain_attn = lax.optimization_barrier(jnp.sum(grad_first * unit_first, axis=0))
    grad_in = grad_middle + norm_back(grad_first, gain_attn.astype(jnp.float32), unit_first, scale_first)
    grads = (grad_gain_attn, grad_qkv, grad_out, grad_gain_mlp, grad_gate_up, grad_down)
    return (result, grad_in, grads)

def reference(hidden_in, cotangent, lengths, gain_attn, w_qkv, w_out, gain_mlp, w_gate_up, w_down):
    inputs = hidden_in.reshape(GROUPS, GRP, D)
    cot_groups = cotangent.reshape(GROUPS, GRP, D)

    def step_group(totals, member):
        group_in, group_cot, length = member
        result, grad_in, grads = layer_group(group_in, group_cot, length, gain_attn, w_qkv, w_out, gain_mlp, w_gate_up, w_down)
        return (jax.tree.map(jnp.add, totals, grads), (result, grad_in))
    start_sums = (jnp.zeros((D,), jnp.float32), jnp.zeros((3, D, D), jnp.float32), jnp.zeros((D, D), jnp.float32), jnp.zeros((D,), jnp.float32), jnp.zeros((D, 2, FF), jnp.float32), jnp.zeros((FF, D), jnp.float32))
    totals, (results, grad_rows) = lax.scan(step_group, start_sums, (inputs, cot_groups, lengths.astype(jnp.int32)))
    return (results.reshape(GROUPS * GRP, D), grad_rows.reshape(GROUPS * GRP, D), totals[0], totals[1], totals[2], totals[3], totals[4], totals[5])
```

```python
import math

import jax
import jax.numpy as jnp
from jax import lax
from jax.sharding import PartitionSpec as P

HEAD_DIM = 96
NORM_EPS = 1e-05
ROPE_BASE = 10000.0
AXES = ("dp", "tensor")
PAIR = 2
NEAR = 1

bf16 = jnp.bfloat16
f32 = jnp.float32


def rotate(values):
    half_width = values.shape[-1] // 2
    return jnp.concatenate([-values[..., half_width:], values[..., :half_width]], axis=-1)


def rotate_back(values):
    half_width = values.shape[-1] // 2
    return jnp.concatenate([values[..., half_width:], -values[..., :half_width]], axis=-1)


def rms_unit(values):
    scale_inv = lax.rsqrt(jnp.mean(values * values, axis=1, keepdims=True) + NORM_EPS)
    return (values * scale_inv, scale_inv)


def norm_back(grad_normed, gain, unit, scale_inv):
    grad_unit = grad_normed * gain
    return scale_inv * (grad_unit - unit * jnp.mean(grad_unit * unit, axis=1, keepdims=True))


def mix(form, left, right):
    return jnp.einsum(form, left, right, preferred_element_type=f32)


class Wires:
    def __init__(self, dp, tp):
        self.dp, self.tp = dp, tp
        self.order = list(range(0, dp, 2)) + list(range(1, dp, 2))
        self.place = {m: p for p, m in enumerate(self.order)}
        self.far = [m for m in range(0, dp, 2) if not m & PAIR]

    def over_dp(self, value, mask):
        pairs = []
        for d in range(self.dp):
            for t in range(self.tp):
                pairs.append((d * self.tp + t, (d ^ mask) * self.tp + t))
        return lax.ppermute(value, AXES, pairs)

    def over_tensor(self, value, mask):
        pairs = []
        for d in range(self.dp):
            for t in range(self.tp):
                pairs.append((d * self.tp + t, d * self.tp + (t ^ mask)))
        return lax.ppermute(value, AXES, pairs)

    def to_relative(self, value, d):
        width = value.shape[1] // self.dp
        return jnp.concatenate(
            [lax.dynamic_slice_in_dim(value, (d ^ m) * width, width, 1) for m in self.order], axis=1
        )

    def to_absolute(self, value, d):
        width = value.shape[1] // self.dp
        parts = []
        for j in range(self.dp):
            m = d ^ j
            place = (m >> 1) + (self.dp // 2) * (m & 1)
            parts.append(lax.dynamic_slice_in_dim(value, place * width, width, 1))
        return jnp.concatenate(parts, axis=1)

    def swap_pair(self, value):
        width = value.shape[1] // self.dp
        parts = []
        for m in self.order:
            p = self.place[m ^ PAIR]
            parts.append(value[:, p * width : (p + 1) * width])
        return jnp.concatenate(parts, axis=1)

    def gather_rows(self, value):
        by_z = self.over_dp(self.swap_pair(value), PAIR)
        by_y = self.over_tensor(value, 2)
        by_zy = self.over_tensor(by_z, 2)
        parts = []
        for part in (value, by_y, by_z, by_zy):
            parts += [part, self.over_tensor(part, 1)]
        return jnp.concatenate(parts, axis=0)

    def sum_rows(self, value):
        rows = value.shape[0] // 8
        blocks = value.reshape(4, 2, rows, value.shape[1])
        halves = []
        for q in range(4):
            got = self.over_tensor(blocks[q, 1].astype(bf16), 1)
            halves.append(blocks[q, 0].astype(f32) + got.astype(f32))
        own, by_y, by_z, by_zy = halves
        got = self.over_tensor(by_zy.astype(bf16), 2)
        by_z = self.swap_pair((by_z + got.astype(f32)).astype(bf16))
        total = own + self.over_tensor(by_y.astype(bf16), 2).astype(f32)
        return total + self.over_dp(by_z, PAIR).astype(f32)

    def gather_weight(self, own, other):
        blocks = {0: own}
        for f in self.far:
            if f:
                blocks[f] = self.over_dp(own, f)
            blocks[f ^ PAIR] = self.over_dp(other, f ^ PAIR)
        for m in list(blocks):
            blocks[m ^ NEAR] = self.over_dp(blocks[m], NEAR)
        return blocks

    def sum_weight(self, even, odd):
        totals = {}
        for m in odd:
            e = m ^ NEAR
            totals[e] = (even[e] + self.over_dp(odd[m].astype(bf16), NEAR).astype(f32)).astype(bf16)
        own = totals[0].astype(f32)
        other = None
        for f in self.far:
            if f:
                own = own + self.over_dp(totals[f], f).astype(f32)
            got = self.over_dp(totals[f ^ PAIR], f ^ PAIR).astype(f32)
            other = got if other is None else other + got
        return own, other


def halves(value, side, axis):
    width = value.shape[axis] // 2
    own = lax.dynamic_slice_in_dim(value, side * width, width, axis)
    other = lax.dynamic_slice_in_dim(value, (1 - side) * width, width, axis)
    return own, other


def joined(own, other, side, axis):
    low = jnp.where(side == 0, own, other)
    high = jnp.where(side == 0, other, own)
    return jnp.concatenate([low, high], axis=axis)


def held_until(value, *waited):
    return lax.optimization_barrier((value, waited))[0]


def on_device(dp, tp, hidden_in, cotangent, lengths, gain_attn, w_qkv, w_out, gain_mlp, w_gate_up, w_down):
    wires = Wires(dp, tp)
    order = wires.order
    half = dp // 2
    d = lax.axis_index("dp")
    t = lax.axis_index("tensor")
    side = (d // PAIR) % 2
    local_rows, width = hidden_in.shape
    group_rows = local_rows * tp
    kb = width // dp
    head_count = w_qkv.shape[2] // HEAD_DIM // 2
    heads = (2, group_rows, head_count, HEAD_DIM)

    pair_gain = jnp.stack([gain_attn, gain_mlp])
    gain_parts = [pair_gain if m == 0 else wires.over_dp(pair_gain, m) for m in order]
    gains = jnp.concatenate(gain_parts, axis=1).astype(f32)
    gain_a, gain_m = gains[0:1], gains[1:2]
    own_length = lengths[0]
    pair_length = wires.over_dp(lengths, PAIR)[0]

    qkv_halves = halves(w_qkv, side, 2)
    out_halves = halves(w_out, side, 0)
    down_halves = halves(w_down, side, 0)
    gu = jnp.transpose(w_gate_up, (1, 0, 2))
    gu_own, gu_other = halves(gu, side, 2)

    b_qkv = wires.gather_weight(*qkv_halves)
    b_out = wires.gather_weight(*held_until(out_halves, b_qkv[PAIR]))
    b_down = wires.gather_weight(*held_until(down_halves, b_out[PAIR], b_qkv[PAIR ^ wires.far[-1]]))
    ff = gu_own.shape[2]
    cut = ff // 2
    b_gu = []
    waited = (b_down[PAIR], b_out[PAIR ^ wires.far[-1]])
    for k in range(2):
        piece = (gu_own[:, :, k * cut : (k + 1) * cut], gu_other[:, :, k * cut : (k + 1) * cut])
        b_gu.append(wires.gather_weight(*held_until(piece, *waited)))
        waited = (b_gu[-1][PAIR], b_down[PAIR ^ wires.far[-1]])

    full_qkv = jnp.concatenate([b_qkv[m] for m in order], axis=1)
    full_out = jnp.concatenate([b_out[m] for m in order], axis=1)
    full_down = jnp.concatenate([b_down[m] for m in order], axis=1)
    full_gu = [jnp.concatenate([b[m] for m in order], axis=1) for b in b_gu]

    starts = jnp.stack([(t ^ q) * local_rows for q in range(tp)])
    positions = (starts[:, None] + jnp.arange(local_rows, dtype=jnp.int32)[None, :]).reshape(-1)
    exponent = jnp.arange(HEAD_DIM // 2).astype(f32) * (2.0 / HEAD_DIM)
    frequency = ROPE_BASE ** (-exponent)
    angles = positions.astype(f32)[:, None] * frequency[None, :]
    cosine = jnp.concatenate([jnp.cos(angles), jnp.cos(angles)], axis=1)[None, :, None, :]
    sine = jnp.concatenate([jnp.sin(angles), jnp.sin(angles)], axis=1)[None, :, None, :]
    live_all = jnp.stack([positions < own_length, positions < pair_length])
    own_rows = t * local_rows + jnp.arange(local_rows, dtype=jnp.int32)
    live = (own_rows < own_length).astype(f32)[:, None]
    allowed = (positions[None, None, :] <= positions[None, :, None]) & (
        live_all[:, :, None] == live_all[:, None, :]
    )

    input_f = wires.to_relative(hidden_in, d).astype(f32)
    unit_first, scale_first = rms_unit(input_f)
    normed_first = wires.gather_rows((unit_first * gain_a).astype(bf16))
    projected = mix("td,jde->jte", normed_first, full_qkv)
    query_raw = projected[0].reshape(heads)
    key_raw = projected[1].reshape(heads)
    queries = (query_raw * cosine + rotate(query_raw) * sine).astype(bf16)
    keys = (key_raw * cosine + rotate(key_raw) * sine).astype(bf16)
    values = projected[2].reshape(heads).astype(bf16)
    scale = 1.0 / math.sqrt(HEAD_DIM)
    scores = mix("gqhd,gkhd->ghqk", queries, keys) * scale
    scores = jnp.where(allowed[:, None], scores, -jnp.inf)
    row_max = jnp.max(scores, axis=3, keepdims=True)
    log_total = row_max + jnp.log(jnp.sum(jnp.exp(scores - row_max), axis=3, keepdims=True))
    attn_prob = jnp.exp(scores - log_total).astype(bf16)
    mixed = mix("ghqk,gkhd->gqhd", attn_prob, values).astype(bf16)
    attn_flat = mixed.reshape(2 * group_rows, -1)
    middle = input_f + wires.sum_rows(jnp.dot(attn_flat, full_out, preferred_element_type=f32).astype(bf16))

    grad_rows = wires.to_relative(cotangent, d) * live
    unit_second, scale_second = rms_unit(middle)
    normed_second = wires.gather_rows((unit_second * gain_m).astype(bf16))
    grad_half = wires.gather_rows(grad_rows.astype(bf16))
    grad_act = jnp.dot(grad_half, full_down.T, preferred_element_type=f32)

    acts, grads_gu, gu_sums, second = [], [], [], None
    cols_even = slice(0, half * kb)
    cols_odd = slice(half * kb, None)

    def row_blocks(big, masks, axis):
        out = {}
        for i, m in enumerate(masks):
            out[m] = lax.slice_in_dim(big, i * kb, (i + 1) * kb, axis=axis)
        return out

    evens, odds = order[:half], order[half:]
    for k in range(2):
        gate_up = mix("td,jdf->jtf", normed_second, full_gu[k])
        gate, up = gate_up[0], gate_up[1]
        sig = jax.nn.sigmoid(gate)
        acts.append((gate * sig * up).astype(bf16))
        ga = grad_act[:, k * cut : (k + 1) * cut]
        g = jnp.stack([ga * up * sig * (1.0 + gate * (1.0 - sig)), ga * gate * sig]).astype(bf16)
        grads_gu.append(g)
        part = mix("jtf,jdf->td", g, full_gu[k])
        second = part if second is None else second + part
    activated = jnp.concatenate(acts, axis=1)

    down_odd = jnp.dot(activated.T, grad_half[:, cols_odd], preferred_element_type=f32).astype(bf16)
    down_even = jnp.dot(activated.T, grad_half[:, cols_even], preferred_element_type=f32)
    sum_down = wires.sum_weight(row_blocks(down_even, evens, 1), row_blocks(down_odd, odds, 1))
    for k in range(2):
        g_odd = mix("td,jtf->jdf", normed_second[:, cols_odd], grads_gu[k]).astype(bf16)
        g_even = mix("td,jtf->jdf", normed_second[:, cols_even], grads_gu[k])
        gu_sums.append(wires.sum_weight(row_blocks(g_even, evens, 1), row_blocks(g_odd, odds, 1)))

    grad_second = wires.sum_rows(second.astype(bf16))
    part_gain_mlp = jnp.sum(grad_second * unit_second, axis=0)
    grad_middle = grad_rows + norm_back(grad_second, gain_m, unit_second, scale_second)
    middle_half = wires.gather_rows(grad_middle.astype(bf16))

    mlp = wires.sum_rows(jnp.dot(activated, full_down, preferred_element_type=f32).astype(bf16))
    layer_out = wires.to_absolute((middle + mlp) * live, d)

    out_odd = jnp.dot(attn_flat.T, middle_half[:, cols_odd], preferred_element_type=f32).astype(bf16)
    out_even = jnp.dot(attn_flat.T, middle_half[:, cols_even], preferred_element_type=f32)
    sum_out = wires.sum_weight(row_blocks(out_even, evens, 1), row_blocks(out_odd, odds, 1))
    grad_mixed = (
        jnp.dot(middle_half, full_out.T, preferred_element_type=f32).astype(bf16).reshape(heads)
    )
    delta = jnp.sum(grad_mixed.astype(f32) * mixed.astype(f32), axis=3)
    delta = jnp.transpose(delta, (0, 2, 1))[..., None]
    prob_full = jnp.exp(scores - log_total)
    grad_prob = mix("gqhd,gkhd->ghqk", grad_mixed, values)
    grad_score = (prob_full * (grad_prob - delta) * scale).astype(bf16)
    grad_query = mix("ghqk,gkhd->gqhd", grad_score, keys)
    grad_keys = mix("ghqk,gqhd->gkhd", grad_score, queries)
    grad_values = mix("ghqk,gqhd->gkhd", prob_full.astype(bf16), grad_mixed)
    query_back = grad_query * cosine + rotate_back(grad_query * sine)
    key_back = grad_keys * cosine + rotate_back(grad_keys * sine)
    grad_proj = (
        jnp.stack([query_back, key_back, grad_values]).astype(bf16).reshape(3, 2 * group_rows, -1)
    )
    q_odd = mix("td,jte->jde", normed_first[:, cols_odd], grad_proj).astype(bf16)
    q_even = mix("td,jte->jde", normed_first[:, cols_even], grad_proj)
    sum_qkv = wires.sum_weight(row_blocks(q_even, evens, 1), row_blocks(q_odd, odds, 1))
    grad_first = wires.sum_rows(mix("jte,jde->td", grad_proj, full_qkv).astype(bf16))
    part_gain_attn = jnp.sum(grad_first * unit_first, axis=0)
    grad_in = grad_middle + norm_back(grad_first, gain_a, unit_first, scale_first)
    grad_in = wires.to_absolute(grad_in, d)

    parts = jnp.stack([part_gain_attn, part_gain_mlp]).reshape(2, dp, kb)
    total = parts[:, wires.place[0]]
    for m in order:
        if m:
            total = total + wires.over_dp(parts[:, wires.place[m]], m)
    for mask in (1, 2):
        total = total + wires.over_tensor(total, mask)

    gu_own = jnp.concatenate([s[0] for s in gu_sums], axis=2)
    gu_other = jnp.concatenate([s[1] for s in gu_sums], axis=2)
    return (
        layer_out,
        grad_in,
        total[0],
        joined(*sum_qkv, side, 2),
        joined(*sum_out, side, 0),
        total[1],
        jnp.transpose(joined(gu_own, gu_other, side, 2), (1, 0, 2)),
        joined(*sum_down, side, 0),
    )


def solution(mesh):
    placed = (
        P(("dp", "tensor"), None),
        P(("dp", "tensor"), None),
        P("dp"),
        P("dp"),
        P(None, "dp", "tensor"),
        P("tensor", "dp"),
        P("dp"),
        P("dp", None, "tensor"),
        P("tensor", "dp"),
    )
    dp, tp = mesh.shape["dp"], mesh.shape["tensor"]

    def body(*args):
        return on_device(dp, tp, *args)

    return jax.shard_map(
        body,
        mesh=mesh,
        in_specs=placed,
        out_specs=(
            P(("dp", "tensor"), None),
            P(("dp", "tensor"), None),
            P("dp"),
            P(None, "dp", "tensor"),
            P("tensor", "dp"),
            P("dp"),
            P("dp", None, "tensor"),
            P("tensor", "dp"),
        ),
        check_vma=False,
    )
```

```python
import math

import jax
import jax.numpy as jnp
from jax import lax
from jax.experimental import pallas as pl
from jax.experimental.pallas import tpu as pltpu
from jax.sharding import PartitionSpec as P

HEAD_DIM = 96
NORM_EPS = 1e-05
ROPE_BASE = 10000.0
AXES = ("dp", "tensor")
PAIR = 2
NEAR = 1
NEGATIVE = -1e30

bf16 = jnp.bfloat16
f32 = jnp.float32


def rms_unit(values):
    scale_inv = lax.rsqrt(jnp.mean(values * values, axis=1, keepdims=True) + NORM_EPS)
    return (values * scale_inv, scale_inv)


def norm_back(grad_normed, gain, unit, scale_inv):
    grad_unit = grad_normed * gain
    return scale_inv * (grad_unit - unit * jnp.mean(grad_unit * unit, axis=1, keepdims=True))


def mix(form, left, right):
    return jnp.einsum(form, left, right, preferred_element_type=f32)


def held_until(value, *waited):
    return lax.optimization_barrier((value, waited))[0]


def dot_last(a, b):
    return lax.dot_general(a, b, (((1,), (1,)), ((), ())), preferred_element_type=f32)


def dot_first(a, b):
    return lax.dot_general(a, b, (((0,), (0,)), ((), ())), preferred_element_type=f32)


def turned(u, low):
    width = u.shape[1]
    half = HEAD_DIM // 2
    return jnp.where(low, pltpu.roll(u, width - half, 1), pltpu.roll(u, half, 1))


def low_lanes(shape):
    lane = lax.broadcasted_iota(jnp.int32, shape, 1)
    low = lane < 0
    for h in range(shape[1] // HEAD_DIM):
        low = low | ((lane >= h * HEAD_DIM) & (lane < h * HEAD_DIM + HEAD_DIM // 2))
    return low


def group_block(ref):
    v = ref[...]
    return v.reshape(v.shape[0] * v.shape[2], v.shape[3])


def put_block(ref, v):
    ref[...] = v.reshape(ref.shape)


def masked_scores(qh, kh, allowed):
    return jnp.where(allowed, dot_last(qh, kh) * (1.0 / math.sqrt(HEAD_DIM)), NEGATIVE)


def allowed_pairs(rows_ref, cols_ref, length):
    rp, cp = rows_ref[...], cols_ref[...]
    return (cp <= rp) & ((rp < length) == (cp < length))


def attend_kernel(len_ref, rows_ref, cols_ref, cos_ref, sin_ref, q_ref, k_ref, v_ref,
                  o_ref, qo_ref, ko_ref, vo_ref, lse_ref):
    allowed = allowed_pairs(rows_ref, cols_ref, len_ref[pl.program_id(0)])
    cosine, sine = cos_ref[...], sin_ref[...]
    low = low_lanes(cosine.shape)
    q, k = group_block(q_ref), group_block(k_ref)
    q = q * cosine + turned(q, low) * sine
    k = k * cosine + turned(k, low) * sine
    v = group_block(v_ref)
    put_block(qo_ref, q.astype(bf16))
    put_block(ko_ref, k.astype(bf16))
    put_block(vo_ref, v.astype(bf16))
    outs, totals = [], []
    for h in range(q.shape[1] // HEAD_DIM):
        c = slice(h * HEAD_DIM, (h + 1) * HEAD_DIM)
        s = masked_scores(q[:, c].astype(bf16), k[:, c].astype(bf16), allowed)
        top = jnp.max(s, axis=1, keepdims=True)
        e = jnp.exp(s - top)
        total = jnp.sum(e, axis=1, keepdims=True)
        prob = (e * (1.0 / total)).astype(bf16)
        outs.append(jnp.dot(prob, v[:, c].astype(bf16), preferred_element_type=f32))
        totals.append(top + jnp.log(total))
    put_block(o_ref, jnp.concatenate(outs, axis=1).astype(bf16))
    put_block(lse_ref, jnp.concatenate(totals, axis=1))


def attend_back_kernel(len_ref, rows_ref, cols_ref, cos_ref, sin_ref, q_ref, k_ref, v_ref, o_ref, g_ref, lse_ref,
                       dq_ref, dk_ref, dv_ref):
    allowed = allowed_pairs(rows_ref, cols_ref, len_ref[pl.program_id(0)])
    q, k, v, g = (group_block(r).astype(f32) for r in (q_ref, k_ref, v_ref, g_ref))
    go = g * group_block(o_ref).astype(f32)
    totals = group_block(lse_ref)
    dqs, dks, dvs = [], [], []
    for h in range(q.shape[1] // HEAD_DIM):
        c = slice(h * HEAD_DIM, (h + 1) * HEAD_DIM)
        qh, kh, vh, gh = (u[:, c].astype(bf16) for u in (q, k, v, g))
        delta = jnp.sum(go[:, c], axis=1, keepdims=True)
        prob = jnp.exp(masked_scores(qh, kh, allowed) - totals[:, h : h + 1])
        ds = (prob * (dot_last(gh, vh) - delta) * (1.0 / math.sqrt(HEAD_DIM))).astype(bf16)
        dqs.append(jnp.dot(ds, kh, preferred_element_type=f32))
        dks.append(dot_first(ds, qh))
        dvs.append(dot_first(prob.astype(bf16), gh))
    cosine, sine = cos_ref[...], sin_ref[...]
    low = low_lanes(cosine.shape)
    for ref, parts in ((dq_ref, dqs), (dk_ref, dks)):
        u = jnp.concatenate(parts, axis=1)
        put_block(ref, (u * cosine - turned(u, low) * sine).astype(bf16))
    put_block(dv_ref, jnp.concatenate(dvs, axis=1).astype(bf16))


def _specs(group_rows, cols, lanes):
    tall = pl.BlockSpec((2, 1, group_rows // 2, cols), lambda g: (0, g, 0, 0))
    table = pl.BlockSpec((group_rows, cols), lambda g: (0, 0))
    head = [
        pl.BlockSpec(memory_space=pltpu.SMEM),
        pl.BlockSpec((group_rows, 1), lambda g: (0, 0)),
        pl.BlockSpec((1, group_rows), lambda g: (0, 0)),
        table,
        table,
    ]
    return head, tall, pl.BlockSpec((2, 1, group_rows // 2, lanes), lambda g: (0, g, 0, 0))


def attend(lengths, positions, cosine, sine, q, k, v):
    rows, cols = q.shape
    half = rows // 4
    lanes = cols // HEAD_DIM
    head, tall, thin = _specs(rows // 2, cols, lanes)
    shape = (2, 2, half, cols)
    outs = pl.pallas_call(
        attend_kernel,
        grid=(2,),
        in_specs=head + [tall] * 3,
        out_specs=[tall] * 4 + [thin],
        out_shape=[jax.ShapeDtypeStruct(shape, bf16)] * 4 + [jax.ShapeDtypeStruct((2, 2, half, lanes), f32)],
        compiler_params=pltpu.CompilerParams(vmem_limit_bytes=48 << 20),
        cost_estimate=pl.CostEstimate(flops=4 * rows * rows * cols // 2, bytes_accessed=rows * cols * 20, transcendentals=rows * rows * lanes // 2),
        name="attend",
    )(lengths, positions[:, None], positions[None, :], cosine, sine, *(u.reshape(shape) for u in (q, k, v)))
    return outs


def attend_back(lengths, positions, cosine, sine, saved, g):
    o, q, k, v, lse = saved
    shape = q.shape
    _, _, half, cols = shape
    rows = 4 * half
    lanes = cols // HEAD_DIM
    head, tall, thin = _specs(rows // 2, cols, lanes)
    outs = pl.pallas_call(
        attend_back_kernel,
        grid=(2,),
        in_specs=head + [tall] * 5 + [thin],
        out_specs=[tall] * 3,
        out_shape=[jax.ShapeDtypeStruct(shape, bf16)] * 3,
        compiler_params=pltpu.CompilerParams(vmem_limit_bytes=48 << 20),
        cost_estimate=pl.CostEstimate(flops=10 * rows * rows * cols // 2, bytes_accessed=rows * cols * 16, transcendentals=rows * rows * lanes // 2),
        name="attend_back",
    )(lengths, positions[:, None], positions[None, :], cosine, sine, q, k, v, o, g.reshape(shape), lse)
    return [u.reshape(rows, cols) for u in outs]


class Wires:
    def __init__(self, dp, tp):
        self.dp, self.tp = dp, tp
        self.order = list(range(0, dp, 2)) + list(range(1, dp, 2))
        self.far = []
        bit = 2 * PAIR
        while bit < dp:
            self.far.append(bit)
            bit *= 2

    def over_dp(self, value, mask):
        pairs = []
        for d in range(self.dp):
            for t in range(self.tp):
                pairs.append((d * self.tp + t, (d ^ mask) * self.tp + t))
        return lax.ppermute(value, AXES, pairs)

    def over_tensor(self, value, mask):
        pairs = []
        for d in range(self.dp):
            for t in range(self.tp):
                pairs.append((d * self.tp + t, d * self.tp + (t ^ mask)))
        return lax.ppermute(value, AXES, pairs)

    def to_relative(self, value, d):
        width = value.shape[1] // self.dp
        return jnp.concatenate(
            [lax.dynamic_slice_in_dim(value, (d ^ m) * width, width, 1) for m in self.order], axis=1
        )

    def to_absolute(self, value, d):
        width = value.shape[1] // self.dp
        parts = []
        for j in range(self.dp):
            m = d ^ j
            place = (m >> 1) + (self.dp // 2) * (m & 1)
            parts.append(lax.dynamic_slice_in_dim(value, place * width, width, 1))
        return jnp.concatenate(parts, axis=1)

    def swap_pair(self, value):
        width = value.shape[1] // self.dp
        parts = []
        for p in range(self.dp):
            q = p ^ 1
            parts.append(value[:, q * width : (q + 1) * width])
        return jnp.concatenate(parts, axis=1)


def halves(value, side, axis):
    width = value.shape[axis] // 2
    own = lax.dynamic_slice_in_dim(value, side * width, width, axis)
    other = lax.dynamic_slice_in_dim(value, (1 - side) * width, width, axis)
    return own, other


def joined(own, other, side, axis):
    low = jnp.where(side == 0, own, other)
    high = jnp.where(side == 0, other, own)
    return jnp.concatenate([low, high], axis=axis)


class Chain:
    def __init__(self):
        self.last = ()

    def pin(self, *values):
        return lax.optimization_barrier((values, self.last))[0]

    def wait(self, *values):
        self.last = self.pin(*values)
        return self.last if len(values) > 1 else self.last[0]

    def step(self, function, *values):
        out = function(*self.pin(*values))
        self.last = out
        return out


class Piece:
    def __init__(self, wires, chain, own, other):
        self.wires, self.chain, self.blocks, self.other = wires, chain, own, other

    def start1(self):
        self.got = self.wires.over_dp(*self.chain.pin(self.other), PAIR)

    def wait1(self):
        self.blocks = jnp.concatenate([self.blocks, self.chain.wait(self.got)], axis=0)

    def start2(self):
        self.got = self.wires.over_dp(*self.chain.pin(self.blocks), self.wires.far[0])

    def wait2(self):
        self.blocks = jnp.concatenate([self.blocks, self.chain.wait(self.got)], axis=0)
        for bit in self.wires.far[1:]:
            got = self.chain.wait(self.wires.over_dp(self.blocks, bit))
            self.blocks = jnp.concatenate([self.blocks, got], axis=0)

    def start3(self):
        self.got = self.wires.over_dp(*self.chain.pin(self.blocks), NEAR)

    def wait3(self):
        self.pair = (self.blocks, self.chain.wait(self.got))

    def full(self):
        return jnp.concatenate(self.pair, axis=0)


class Grad:
    def __init__(self, wires, chain, x, y):
        self.wires, self.chain, self.x, self.y = wires, chain, x, y

    def part(self, x, y, low, high):
        return mix("tk,tn->kn", x[:, low:high], y)

    def odd(self):
        k = self.x.shape[1] // 2
        self.send = self.chain.step(lambda x, y: self.part(x, y, k, 2 * k).astype(bf16), self.x, self.y)

    def start1(self):
        self.got = self.wires.over_dp(*self.chain.pin(self.send), NEAR)

    def wait1(self):
        got = self.chain.wait(self.got)
        k = self.x.shape[1] // 2
        h = k // 2

        def far_half(x, y, g):
            return (self.part(x, y, h, k) + g[h:].astype(f32)).astype(bf16)

        def near_half(x, y, g):
            return self.part(x, y, 0, h) + g[:h].astype(f32)

        self.send = self.chain.step(far_half, self.x, self.y, got)
        self.got = self.wires.over_dp(self.send, self.wires.far[-1])
        self.keep = self.chain.step(near_half, self.x, self.y, got)

    def wait2(self):
        got = self.chain.wait(self.got)
        for bit in reversed(self.wires.far[:-1]):
            total = self.keep + got.astype(f32)
            rows = total.shape[0] // 2
            self.keep = total[:rows]
            got = self.chain.wait(self.wires.over_dp(total[rows:].astype(bf16), bit))
        rows = got.shape[0] // 2

        def add(keep, g):
            total = keep + g.astype(f32)
            return total[:rows], total[rows:].astype(bf16)

        self.own, send = self.chain.step(add, self.keep, got)
        self.got = self.wires.over_dp(send, PAIR)

    def wait3(self):
        self.other = self.chain.wait(self.got)


class RowGather:
    def __init__(self, wires, chain, value, swapped):
        self.wires, self.chain, self.value = wires, chain, value
        value, swapped = chain.pin(value, swapped)
        self.z = wires.over_dp(swapped, PAIR)
        self.y = wires.over_tensor(value, 2)

    def wait1(self):
        self.z = self.chain.wait(self.z)
        self.zy = self.wires.over_tensor(self.z, 2)

    def wait2(self):
        self.y = self.chain.wait(self.y)
        self.first = self.chain.step(
            lambda v, y, z: jnp.concatenate([v, y, z], axis=0), self.value, self.y, self.z
        )
        self.c = self.wires.over_tensor(self.first, 1)

    def wait3(self):
        self.zy = self.chain.wait(self.zy)
        self.czy = self.wires.over_tensor(self.zy, 1)

    def wait4(self):
        c, czy = self.chain.wait(self.c, self.czy)
        return self.chain.step(lambda *v: jnp.concatenate(v, axis=0), self.first, self.zy, c, czy)


class RowSum:
    def __init__(self, wires, chain, value):
        self.wires, self.chain = wires, chain
        self.rows = value.shape[0] // 8
        self.near, far = chain.step(lambda v: (v[: 4 * self.rows], v[4 * self.rows :]), value)
        self.c = wires.over_tensor(far, 1)

    def wait1(self):
        got = self.chain.wait(self.c)
        rows = self.rows

        def last(near, g):
            return (near[3 * rows :].astype(f32) + g[3 * rows :].astype(f32)).astype(bf16)

        def rest(near, g):
            total = near[: 3 * rows].astype(f32) + g[: 3 * rows].astype(f32)
            return total[:rows], total[rows : 2 * rows].astype(bf16), total[2 * rows :]

        self.zy = self.wires.over_tensor(self.chain.step(last, self.near, got), 2)
        self.own, y, self.z = self.chain.step(rest, self.near, got)
        self.y = self.wires.over_tensor(y, 2)

    def wait2(self):
        got = self.chain.wait(self.zy)
        z = self.chain.step(lambda z, g: self.wires.swap_pair((z + g.astype(f32)).astype(bf16)), self.z, got)
        self.z = self.wires.over_dp(z, PAIR)

    def wait3(self):
        self.y, self.z = self.chain.wait(self.y, self.z)


def on_device(dp, tp, hidden_in, cotangent, lengths, gain_attn, w_qkv, w_out, gain_mlp, w_gate_up, w_down):
    wires = Wires(dp, tp)
    chain = Chain()
    d = lax.axis_index("dp")
    t = lax.axis_index("tensor")
    side = (d // PAIR) % 2
    local_rows, width = hidden_in.shape
    group_rows = local_rows * tp
    kb = width // dp
    cols = w_qkv.shape[2] // 2
    head_count = cols // HEAD_DIM

    pieces = [Piece(wires, chain, *halves(w_qkv[j], side, 1)) for j in range(3)]
    pieces.append(Piece(wires, chain, *[h.T for h in halves(w_out, side, 0)]))
    down_own, down_other = (h.T for h in halves(w_down, side, 0))
    ff = down_own.shape[1]
    n_down, n_gu = 2, 4
    cut = ff // n_down
    for k in range(n_down):
        pieces.append(Piece(wires, chain, *[h[:, k * cut : (k + 1) * cut] for h in (down_own, down_other)]))
    gu_own, gu_other = halves(w_gate_up, side, 2)
    cg = ff // n_gu
    for k in range(n_gu):
        pieces.append(
            Piece(wires, chain, *[h[:, :, k * cg : (k + 1) * cg].reshape(kb, 2 * cg) for h in (gu_own, gu_other)])
        )
    w_q, w_k, w_v, w_o, d0, d1, g0, g1, g2, g3 = pieces
    gus = [g0, g1, g2, g3]

    w_q.start1()
    gains = jnp.stack([gain_attn, gain_mlp])[:, None]
    w_k.start1()
    pair_length = wires.over_dp(lengths, PAIR)
    got = wires.over_dp(gains, PAIR)
    w_q.wait1()
    w_q.start2()
    for bit in wires.far + [NEAR]:
        gains = jnp.concatenate([gains, chain.wait(got)], axis=1)
        got = wires.over_dp(gains, bit)
    gains = jnp.concatenate([gains, chain.wait(got)], axis=1)
    gains = gains.reshape(2, width).astype(f32)
    gain_a, gain_m = gains[0:1], gains[1:2]

    def open_rows(x, gain):
        x = wires.to_relative(x, d).astype(f32)
        unit, scale = rms_unit(x)
        v = (unit * gain).astype(bf16)
        return x, unit, scale, v, wires.swap_pair(v)

    input_f, unit_first, scale_first, v, swapped = chain.step(open_rows, hidden_in, gain_a)
    rows_a = RowGather(wires, chain, v, swapped)
    w_k.wait1()
    w_k.start2()
    w_v.start1()

    def tables(lengths, pair_length):
        starts = jnp.stack([t, t ^ 2, t ^ 1, t ^ 3]) * local_rows
        positions = (starts[:, None] + jnp.arange(local_rows, dtype=jnp.int32)[None, :]).reshape(-1)
        exponent = jnp.arange(HEAD_DIM // 2).astype(f32) * (2.0 / HEAD_DIM)
        frequency = ROPE_BASE ** (-exponent)
        angles = positions.astype(f32)[:, None] * frequency[None, :]
        cosine = jnp.tile(jnp.concatenate([jnp.cos(angles), jnp.cos(angles)], axis=1), (1, head_count))
        sine = jnp.tile(jnp.concatenate([-jnp.sin(angles), jnp.sin(angles)], axis=1), (1, head_count))
        return jnp.concatenate([lengths, pair_length]), positions, cosine, sine

    own_rows = t * local_rows + jnp.arange(local_rows, dtype=jnp.int32)
    live = (own_rows < lengths[0]).astype(f32)[:, None]

    def open_cotangent(c, live):
        g = wires.to_relative(c, d) * live
        h = g.astype(bf16)
        return g, h, wires.swap_pair(h)

    grad_rows, gv, gswapped = chain.step(open_cotangent, cotangent, live)
    rows_a.wait1()
    rows_a.wait2()
    w_q.wait2()
    w_q.start3()
    table = chain.step(tables, lengths, pair_length)
    w_v.wait1()
    w_v.start2()
    rows_a.wait3()
    normed_first = rows_a.wait4()
    w_k.wait2()
    w_k.start3()
    w_o.start1()
    rows_g = RowGather(wires, chain, gv, gswapped)

    def product(x, piece):
        k = width // 2
        return chain.step(
            lambda x, e, o: jnp.dot(x[:, :k], e, preferred_element_type=f32)
            + jnp.dot(x[:, k:], o, preferred_element_type=f32),
            x, *piece.pair,
        )

    w_q.wait3()
    query_raw = product(normed_first, w_q)
    w_o.wait1()
    rows_g.wait1()
    w_v.wait2()
    w_v.start3()
    w_o.start2()
    d0.start1()
    rows_g.wait2()
    w_k.wait3()
    key_raw = product(normed_first, w_k)
    d0.wait1()
    w_o.wait2()
    w_o.start3()
    d0.start2()
    d1.start1()
    rows_g.wait3()
    w_v.wait3()
    value_raw = product(normed_first, w_v)
    saved = chain.step(lambda *a: attend(*a), *table, query_raw, key_raw, value_raw)
    attn_flat = saved[0].reshape(2 * group_rows, cols)
    grad_half = rows_g.wait4()
    w_o.wait3()
    back = lambda y, e, o: mix("tn,kn->tk", y, jnp.concatenate([e, o], axis=0)).astype(bf16)
    mixed_out = RowSum(wires, chain, chain.step(back, attn_flat, *w_o.pair))
    d1.wait1()
    d0.wait2()
    d0.start3()
    d1.start2()
    g0.start1()
    mixed_out.wait1()
    g0.wait1()
    mixed_out.wait2()
    d1.wait2()
    d1.start3()
    g0.start2()
    g1.start1()
    d0.wait3()
    act_0 = product(grad_half, d0)
    mixed_out.wait3()

    def open_second(own, y, z, x, gain):
        middle = x + own + y.astype(f32) + z.astype(f32)
        unit, scale = rms_unit(middle)
        v = (unit * gain).astype(bf16)
        return middle, unit, scale, v, wires.swap_pair(v)

    middle, unit_second, scale_second, v, swapped = chain.step(
        open_second, mixed_out.own, mixed_out.y, mixed_out.z, input_f, gain_m
    )
    rows_n = RowGather(wires, chain, v, swapped)
    g1.wait1()
    d1.wait3()
    act_1 = product(grad_half, d1)
    grad_acts = [act_0, act_1]
    rows_n.wait1()
    g0.wait2()
    g0.start3()
    g1.start2()
    g2.start1()
    rows_n.wait2()
    rows_n.wait3()
    g2.wait1()
    normed_second = rows_n.wait4()
    g1.wait2()
    g1.start3()
    g2.start2()
    g3.start1()

    per = n_gu // n_down
    acts, grads_gu, second, grads = [], [], None, []

    def gated(x, e, o, ga):
        k = width // 2
        gate_up = jnp.dot(x[:, :k], e, preferred_element_type=f32) + jnp.dot(
            x[:, k:], o, preferred_element_type=f32
        )
        gate, up = gate_up[:, :cg], gate_up[:, cg:]
        sig = jax.nn.sigmoid(gate)
        g = jnp.concatenate([ga * up * sig * (1.0 + gate * (1.0 - sig)), ga * gate * sig], axis=1)
        return (gate * sig * up).astype(bf16), g.astype(bf16)

    def forward_gu(k):
        ga = grad_acts[k // per][:, (k % per) * cg : (k % per + 1) * cg]
        return chain.step(gated, normed_second, *gus[k].pair, ga)

    def add_second(parts, g, piece, last):
        def one(g, w, part=None):
            out = mix("tn,kn->tk", g, w)
            if part is not None:
                out = out + part
            return out.astype(bf16) if last else out

        if parts is None:
            return [chain.step(one, g, w) for w in piece.pair]
        return [chain.step(one, g, w, p) for w, p in zip(piece.pair, parts)]

    for k in range(n_gu):
        gus[k].wait3()
        act, g = forward_gu(k)
        acts.append(act)
        if k == n_gu - 1:
            grads[0].start1()
        second = add_second(second, g, gus[k], k == n_gu - 1)
        grads.append(Grad(wires, chain, normed_second, g))
        if k < n_gu - 1:
            grads[k].odd()
        if k == 0:
            g3.wait1()
            g2.wait2()
            g2.start3()
            g3.start2()
        if k == 1:
            g3.wait2()
            g3.start3()

    second = chain.step(lambda e, o: jnp.concatenate([e, o], axis=1), *second)
    sum_second = RowSum(wires, chain, second)
    grads[1].start1()
    grads[3].odd()
    sum_second.wait1()
    acts = [jnp.concatenate(acts[k * per : (k + 1) * per], axis=1) for k in range(n_down)]
    grads += [Grad(wires, chain, grad_half, a) for a in acts]
    grads[4].odd()
    grads[5].odd()
    grads[0].wait1()
    grads[2].start1()
    sum_second.wait2()

    def down_product(a0, a1, *w):
        full = [jnp.concatenate(w[:2], axis=0), jnp.concatenate(w[2:], axis=0)]
        return (mix("tn,kn->tk", a0, full[0]) + mix("tn,kn->tk", a1, full[1])).astype(bf16)

    mlp_part = chain.step(down_product, *acts, *d0.pair, *d1.pair)
    grads[1].wait1()
    grads[3].start1()
    sum_second.wait3()
    grads[0].wait2()

    def close_second(own, y, z, gain, unit, scale, rows):
        grad = own + y.astype(f32) + z.astype(f32)
        middle = rows + norm_back(grad, gain, unit, scale)
        h = middle.astype(bf16)
        return jnp.sum(grad * unit, axis=0), middle, h, wires.swap_pair(h)

    part_gain_mlp, grad_middle, v, swapped = chain.step(
        close_second, sum_second.own, sum_second.y, sum_second.z, gain_m, unit_second, scale_second, grad_rows
    )
    rows_m = RowGather(wires, chain, v, swapped)
    grads[2].wait1()
    grads[4].start1()
    rows_m.wait1()
    grads[1].wait2()
    rows_m.wait2()
    grads[0].wait3()
    rows_m.wait3()
    middle_half = rows_m.wait4()
    mlp = RowSum(wires, chain, mlp_part)
    grad_mixed = product(middle_half, w_o).astype(bf16)
    grads[3].wait1()
    grads[5].start1()
    mlp.wait1()
    grad_proj = chain.step(lambda *a: attend_back(*a), *table, saved, grad_mixed)
    grads[2].wait2()
    grads.append(Grad(wires, chain, middle_half, attn_flat))
    grads[6].odd()
    mlp.wait2()
    grads += [Grad(wires, chain, normed_first, g) for g in grad_proj]
    first = None
    for g, w in zip(grad_proj, (w_q, w_k, w_v)):
        first = add_second(first, g, w, w is w_v)
    first = chain.step(lambda e, o: jnp.concatenate([e, o], axis=1), *first)
    mlp.wait3()
    layer_out = chain.step(
        lambda own, y, z, m, live: wires.to_absolute((m + own + y.astype(f32) + z.astype(f32)) * live, d),
        mlp.own, mlp.y, mlp.z, middle, live,
    )
    sum_first = RowSum(wires, chain, first)
    grads[4].wait1()
    grads[6].start1()
    grads[1].wait3()
    grads[7].odd()
    sum_first.wait1()
    grads[3].wait2()
    grads[8].odd()
    sum_first.wait2()
    grads[2].wait3()
    grads[5].wait1()
    grads[7].start1()
    sum_first.wait3()

    def close_first(own, y, z, gain, unit, scale, rows):
        grad = own + y.astype(f32) + z.astype(f32)
        out = rows + norm_back(grad, gain, unit, scale)
        return jnp.sum(grad * unit, axis=0), wires.to_absolute(out, d)

    part_gain_attn, grad_in = chain.step(
        close_first, sum_first.own, sum_first.y, sum_first.z, gain_a, unit_first, scale_first, grad_middle
    )
    grads[9].odd()
    grads[4].wait2()
    grads[3].wait3()

    total = jnp.stack([part_gain_attn, part_gain_mlp]).reshape(2, dp, kb)
    grads[6].wait1()
    grads[8].start1()

    def gain_step(bit):
        nonlocal total
        rows = total.shape[1] // 2
        total = total[:, :rows] + chain.wait(wires.over_dp(total[:, rows:], bit))

    gain_step(NEAR)
    grads[5].wait2()
    grads[4].wait3()
    for bit in wires.far[::-1]:
        gain_step(bit)
    grads[7].wait1()
    grads[9].start1()
    gain_step(PAIR)
    grads[6].wait2()
    grads[5].wait3()
    total = total[:, 0]
    total = total + chain.wait(wires.over_tensor(total, 1))
    grads[8].wait1()
    total = total + chain.wait(wires.over_tensor(total, 2))
    grads[7].wait2()
    grads[6].wait3()
    grads[9].wait1()
    grads[8].wait2()
    grads[7].wait3()
    grads[9].wait2()
    grads[8].wait3()
    grads[9].wait3()

    sides = ([g.own for g in grads], [g.other.astype(f32) for g in grads])

    def down_of(s):
        return jnp.concatenate(s[4:6], axis=1).T

    def gu_of(s):
        return jnp.concatenate([p.reshape(kb, 2, cg) for p in s[:4]], axis=2)

    return (
        layer_out,
        grad_in,
        total[0],
        jnp.stack([joined(sides[0][i], sides[1][i], side, 1) for i in (7, 8, 9)]),
        joined(sides[0][6].T, sides[1][6].T, side, 0),
        total[1],
        joined(gu_of(sides[0]), gu_of(sides[1]), side, 2),
        joined(down_of(sides[0]), down_of(sides[1]), side, 0),
    )


def solution(mesh):
    placed = (
        P(("dp", "tensor"), None),
        P(("dp", "tensor"), None),
        P("dp"),
        P("dp"),
        P(None, "dp", "tensor"),
        P("tensor", "dp"),
        P("dp"),
        P("dp", None, "tensor"),
        P("tensor", "dp"),
    )
    dp, tp = mesh.shape["dp"], mesh.shape["tensor"]

    def body(*args):
        return on_device(dp, tp, *args)

    return jax.shard_map(
        body,
        mesh=mesh,
        in_specs=placed,
        out_specs=(
            P(("dp", "tensor"), None),
            P(("dp", "tensor"), None),
            P("dp"),
            P(None, "dp", "tensor"),
            P("tensor", "dp"),
            P("dp"),
            P("dp", None, "tensor"),
            P("tensor", "dp"),
        ),
        check_vma=False,
    )
```

```python
import math

import jax
import jax.numpy as jnp
from jax import lax
from jax.experimental import pallas as pl
from jax.experimental.pallas import tpu as pltpu
from jax.sharding import PartitionSpec as P

HEAD_DIM = 96
NORM_EPS = 1e-05
ROPE_BASE = 10000.0
AXES = ("dp", "tensor")
PAIR = 2
NEAR = 1
NEGATIVE = -1e30

bf16 = jnp.bfloat16
f32 = jnp.float32


def dot_last(a, b):
    return lax.dot_general(a, b, (((1,), (1,)), ((), ())), preferred_element_type=f32)


def dot_first(a, b):
    return lax.dot_general(a, b, (((0,), (0,)), ((), ())), preferred_element_type=f32)


def turned(u, low):
    width = u.shape[1]
    half = HEAD_DIM // 2
    return jnp.where(low, pltpu.roll(u, width - half, 1), pltpu.roll(u, half, 1))


def low_lanes(shape):
    lane = lax.broadcasted_iota(jnp.int32, shape, 1)
    low = lane < 0
    for h in range(shape[1] // HEAD_DIM):
        low = low | ((lane >= h * HEAD_DIM) & (lane < h * HEAD_DIM + HEAD_DIM // 2))
    return low


def group_block(ref):
    return ref[...]


def put_block(ref, v):
    ref[...] = v


def masked_scores(qh, kh, allowed):
    return jnp.where(allowed, dot_last(qh, kh) * (1.0 / math.sqrt(HEAD_DIM)), NEGATIVE)


def allowed_pairs(rows_ref, cols_ref, length):
    rp, cp = rows_ref[...], cols_ref[...]
    return (cp <= rp) & ((rp < length) == (cp < length))


def attend_kernel(len_ref, rows_ref, cols_ref, cos_ref, sin_ref, q_ref, k_ref, v_ref,
                  o_ref, qo_ref, ko_ref, vo_ref, lse_ref):
    allowed = allowed_pairs(rows_ref, cols_ref, len_ref[pl.program_id(0)])
    cosine, sine = cos_ref[...], sin_ref[...]
    low = low_lanes(cosine.shape)
    q, k = group_block(q_ref), group_block(k_ref)
    q = q * cosine + turned(q, low) * sine
    k = k * cosine + turned(k, low) * sine
    v = group_block(v_ref)
    put_block(qo_ref, q.astype(bf16))
    put_block(ko_ref, k.astype(bf16))
    put_block(vo_ref, v.astype(bf16))
    outs, totals = [], []
    for h in range(q.shape[1] // HEAD_DIM):
        c = slice(h * HEAD_DIM, (h + 1) * HEAD_DIM)
        s = masked_scores(q[:, c].astype(bf16), k[:, c].astype(bf16), allowed)
        top = jnp.max(s, axis=1, keepdims=True)
        e = jnp.exp(s - top)
        total = jnp.sum(e, axis=1, keepdims=True)
        prob = (e * (1.0 / total)).astype(bf16)
        outs.append(jnp.dot(prob, v[:, c].astype(bf16), preferred_element_type=f32))
        totals.append(top + jnp.log(total))
    put_block(o_ref, jnp.concatenate(outs, axis=1).astype(bf16))
    put_block(lse_ref, jnp.concatenate(totals, axis=1))


def attend_back_kernel(len_ref, rows_ref, cols_ref, cos_ref, sin_ref, q_ref, k_ref, v_ref, o_ref, g_ref, lse_ref,
                       dq_ref, dk_ref, dv_ref):
    allowed = allowed_pairs(rows_ref, cols_ref, len_ref[pl.program_id(0)])
    q, k, v, g = (group_block(r).astype(f32) for r in (q_ref, k_ref, v_ref, g_ref))
    go = g * group_block(o_ref).astype(f32)
    totals = group_block(lse_ref)
    dqs, dks, dvs = [], [], []
    for h in range(q.shape[1] // HEAD_DIM):
        c = slice(h * HEAD_DIM, (h + 1) * HEAD_DIM)
        qh, kh, vh, gh = (u[:, c].astype(bf16) for u in (q, k, v, g))
        delta = jnp.sum(go[:, c], axis=1, keepdims=True)
        prob = jnp.exp(masked_scores(qh, kh, allowed) - totals[:, h : h + 1])
        ds = (prob * (dot_last(gh, vh) - delta) * (1.0 / math.sqrt(HEAD_DIM))).astype(bf16)
        dqs.append(jnp.dot(ds, kh, preferred_element_type=f32))
        dks.append(dot_first(ds, qh))
        dvs.append(dot_first(prob.astype(bf16), gh))
    cosine, sine = cos_ref[...], sin_ref[...]
    low = low_lanes(cosine.shape)
    for ref, parts in ((dq_ref, dqs), (dk_ref, dks)):
        u = jnp.concatenate(parts, axis=1)
        put_block(ref, (u * cosine - turned(u, low) * sine).astype(bf16))
    put_block(dv_ref, jnp.concatenate(dvs, axis=1).astype(bf16))


def attend_specs(group_rows, cols, lanes):
    tall = pl.BlockSpec((group_rows, cols), lambda g: (g, 0))
    table = pl.BlockSpec((group_rows, cols), lambda g: (0, 0))
    head = [
        pl.BlockSpec(memory_space=pltpu.SMEM),
        pl.BlockSpec((group_rows, 1), lambda g: (0, 0)),
        pl.BlockSpec((1, group_rows), lambda g: (0, 0)),
        table,
        table,
    ]
    return head, tall, pl.BlockSpec((group_rows, lanes), lambda g: (g, 0))


def attend(lengths, positions, cosine, sine, q, k, v):
    rows, cols = q.shape
    lanes = cols // HEAD_DIM
    head, tall, thin = attend_specs(rows // 2, cols, lanes)
    return run(
        attend_kernel, "attend", [((rows, cols), bf16)] * 4 + [((rows, lanes), f32)],
        [lengths, positions[:, None], positions[None, :], cosine, sine, q, k, v], (2,),
        head + [tall] * 3, [tall] * 4 + [thin],
    )


def attend_back(lengths, positions, cosine, sine, saved, g):
    o, q, k, v, lse = saved
    rows, cols = q.shape
    head, tall, thin = attend_specs(rows // 2, cols, cols // HEAD_DIM)
    return run(
        attend_back_kernel, "attend_back", [((rows, cols), bf16)] * 3,
        [lengths, positions[:, None], positions[None, :], cosine, sine, q, k, v, o, g, lse], (2,),
        head + [tall] * 5 + [thin], [tall] * 3,
    )


def run(kernel, name, outs, args, grid=(), in_specs=None, out_specs=None, scratch=(), scalars=0):
    whole = pl.BlockSpec(memory_space=pltpu.VMEM)
    if in_specs is None:
        in_specs = [whole] * (len(args) - scalars)
    if out_specs is None:
        out_specs = [whole] * len(outs)
    got = pl.pallas_call(
        kernel,
        out_shape=[jax.ShapeDtypeStruct(s, t) for s, t in outs],
        grid_spec=pltpu.PrefetchScalarGridSpec(
            num_scalar_prefetch=scalars, grid=grid, in_specs=in_specs, out_specs=out_specs, scratch_shapes=scratch
        ),
        compiler_params=pltpu.CompilerParams(vmem_limit_bytes=52 << 20),
        cost_estimate=pl.CostEstimate(flops=1, bytes_accessed=1, transcendentals=0),
        name=name,
    )(*args)
    return list(got)


SMALL = pl.BlockSpec(memory_space=pltpu.SMEM)
VMEM = pl.BlockSpec(memory_space=pltpu.VMEM)


def tiles(rows, width):
    return pl.BlockSpec((rows, width), lambda i: (i, 0))


def still(shape):
    return pl.BlockSpec(shape, lambda i: (0,) * len(shape), pipeline_mode=pl.Buffered(1))


def product(x, pair, dtype=f32):
    rows, width = x.shape
    k, n = pair[0].shape
    tile = rows // 4

    def kernel(x_ref, even, odd, out):
        total = jnp.dot(x_ref[:, :k], even[...], preferred_element_type=f32)
        total += jnp.dot(x_ref[:, k:], odd[...], preferred_element_type=f32)
        out[...] = total.astype(dtype)

    return run(
        kernel, "product", [((rows, n), dtype)], [x, *pair], (4,),
        [tiles(tile, width)] + [still((k, n))] * 2, [tiles(tile, n)],
    )[0]


def gated(x, pair, grad_act, column):
    rows, width = x.shape
    k, n = pair[0].shape
    c = n // 2
    tile = rows // 4

    def kernel(x_ref, even, odd, ga_ref, act, grad):
        total = jnp.dot(x_ref[:, :k], even[...], preferred_element_type=f32)
        total += jnp.dot(x_ref[:, k:], odd[...], preferred_element_type=f32)
        gate, up, ga = total[:, :c], total[:, c:], ga_ref[...]
        sig = jax.nn.sigmoid(gate)
        act[...] = (gate * sig * up).astype(bf16)
        grad[:, :c] = (ga * up * sig * (1.0 + gate * (1.0 - sig))).astype(bf16)
        grad[:, c:] = (ga * gate * sig).astype(bf16)

    return run(
        kernel, "gated", [((rows, c), bf16), ((rows, n), bf16)], [x, *pair, grad_act], (4,),
        [tiles(tile, width)] + [still((k, n))] * 2 + [pl.BlockSpec((tile, c), lambda i: (i, column))],
        [tiles(tile, c), tiles(tile, n)],
    )


def back(ys, pairs, dtype, part=None):
    rows = ys[0].shape[0]
    k = pairs[0][0].shape[0]
    count = len(ys)
    tile = rows // 4

    def kernel(*refs):
        y_refs, w_refs, out = refs[:count], refs[count : 3 * count], refs[-1]
        for s in range(2):
            c = slice(s * k, (s + 1) * k)
            total = refs[3 * count][:, c] if part is not None else None
            for y, w in zip(y_refs, w_refs[s::2]):
                term = dot_last(y[...], w[...])
                total = term if total is None else total + term
            out[:, c] = total.astype(dtype)

    flat = [w for p in pairs for w in p]
    return run(
        kernel, "back", [((rows, 2 * k), dtype)], [*ys, *flat] + ([] if part is None else [part]), (4,),
        [tiles(tile, y.shape[1]) for y in ys]
        + [still(w.shape) for w in flat]
        + ([] if part is None else [tiles(tile, 2 * k)]),
        [tiles(tile, 2 * k)],
    )[0]


def weight_part(x, y, first, count, dtype, got=None, got_first=0):
    rows = x.shape[0]
    n = y.shape[1]
    tile = count if count <= 768 else count // 2
    base, got_base = first // tile, got_first // tile

    def kernel(x_ref, y_ref, *rest):
        total = dot_first(x_ref[...], y_ref[...])
        if got is not None:
            total += rest[0][...].astype(f32)
        rest[-1][...] = total.astype(dtype)

    extra = [] if got is None else [pl.BlockSpec((tile, n), lambda i: (i + got_base, 0))]
    return run(
        kernel, "weight_part", [((count, n), dtype)], [x, y] + ([] if got is None else [got]), (count // tile,),
        [pl.BlockSpec((rows, tile), lambda i: (0, i + base)), still(y.shape)] + extra, [tiles(tile, n)],
    )[0]


class Rows:
    def __init__(self, wires, info, rows, width):
        self.wires, self.info, self.rows, self.width = wires, info, rows, width
        self.kb = width // wires.dp
        self.inside = self.kb % 128 == 0

    def load_relative(self, ref, info):
        if not self.inside:
            return ref[...].astype(f32)
        kb = self.kb
        parts = []
        for m in self.wires.order:
            parts.append(ref[:, pl.ds(pl.multiple_of((info[0] ^ m) * kb, 128), kb)].astype(f32))
        return jnp.concatenate(parts, axis=1)

    def store_absolute(self, ref, value, scratch, info):
        if not self.inside:
            ref[...] = value
            return
        kb, half = self.kb, self.wires.dp // 2
        scratch[...] = value
        for j in range(self.wires.dp):
            m = info[0] ^ j
            place = (m >> 1) + half * (m & 1)
            ref[:, j * kb : (j + 1) * kb] = scratch[:, pl.ds(pl.multiple_of(place * kb, 128), kb)]

    def relative(self, x):
        return x if self.inside else self.wires.to_relative(x, self.info[0])

    def absolute(self, x):
        return x if self.inside else self.wires.to_absolute(x, self.info[0])

    def live(self, info, shape):
        row = info[1] * shape[0] + lax.broadcasted_iota(jnp.int32, (shape[0], 1), 0)
        return (row < info[2]).astype(f32)

    def outs(self, *dtypes):
        return [((self.rows, self.width), t) for t in dtypes]

    def open_first(self, x, gains):
        def kernel(info, x_ref, gain_ref, rel, scale_ref, v):
            x = self.load_relative(x_ref, info)
            scale = lax.rsqrt(jnp.mean(x * x, axis=1, keepdims=True) + NORM_EPS)
            rel[...] = x
            scale_ref[...] = scale
            v[...] = (x * scale * gain_ref[0:1].astype(f32)).astype(bf16)

        return run(
            kernel, "open_first", self.outs(f32) + [((self.rows, 1), f32)] + self.outs(bf16),
            [self.info, self.relative(x), gains], in_specs=[SMALL, VMEM, VMEM],
        )

    def open_cotangent(self, c):
        def kernel(info, c_ref, g, v):
            x = self.load_relative(c_ref, info)
            x = x * self.live(info, x.shape)
            g[...] = x
            v[...] = x.astype(bf16)

        return run(
            kernel, "open_cotangent", self.outs(f32, bf16), [self.info, self.relative(c)], in_specs=[SMALL, VMEM]
        )

    def open_second(self, x, got, gains):
        def kernel(x_ref, got_ref, gain_ref, mid, scale_ref, v):
            middle = x_ref[...] + got_ref[...].astype(f32)
            scale = lax.rsqrt(jnp.mean(middle * middle, axis=1, keepdims=True) + NORM_EPS)
            mid[...] = middle
            scale_ref[...] = scale
            v[...] = (middle * scale * gain_ref[1:2].astype(f32)).astype(bf16)

        return run(
            kernel, "open_second", self.outs(f32) + [((self.rows, 1), f32)] + self.outs(bf16), [x, got, gains]
        )

    def norm_back(self, got_ref, gain, x_ref, scale_ref, rows_ref, part):
        grad = got_ref[...].astype(f32)
        scale = scale_ref[...]
        unit = x_ref[...] * scale
        part[...] = jnp.sum(grad * unit, axis=0, keepdims=True)
        e = grad * gain
        return rows_ref[...] + scale * (e - unit * jnp.mean(e * unit, axis=1, keepdims=True))

    def close_second(self, got, gains, middle, scale, rows):
        def kernel(got_ref, gain_ref, x_ref, scale_ref, rows_ref, part, mid, v):
            grad = self.norm_back(got_ref, gain_ref[1:2].astype(f32), x_ref, scale_ref, rows_ref, part)
            mid[...] = grad
            v[...] = grad.astype(bf16)

        return run(
            kernel, "close_second", [((1, self.width), f32)] + self.outs(f32, bf16),
            [got, gains, middle, scale, rows],
        )

    def close_first(self, got, gains, x, scale, rows):
        def kernel(info, got_ref, gain_ref, x_ref, scale_ref, rows_ref, part, out, scratch):
            grad = self.norm_back(got_ref, gain_ref[0:1].astype(f32), x_ref, scale_ref, rows_ref, part)
            self.store_absolute(out, grad, scratch, info)

        part, out = run(
            kernel, "close_first", [((1, self.width), f32)] + self.outs(f32),
            [self.info, got, gains, x, scale, rows], in_specs=[SMALL] + [VMEM] * 5,
            scratch=[pltpu.VMEM((self.rows, self.width), f32)],
        )
        return part, self.absolute(out)

    def close_layer(self, got, middle):
        def kernel(info, got_ref, mid_ref, out, scratch):
            total = mid_ref[...] + got_ref[...].astype(f32)
            self.store_absolute(out, total * self.live(info, total.shape), scratch, info)

        out, = run(
            kernel, "close_layer", self.outs(f32), [self.info, got, middle], in_specs=[SMALL] + [VMEM] * 2,
            scratch=[pltpu.VMEM((self.rows, self.width), f32)],
        )
        return self.absolute(out)


def in_order(side, own, far, far_pair, pair):
    kb, n = own.shape

    def kernel(side_ref, *refs):
        i, s = pl.program_id(0), side_ref[0]
        for at, ref in enumerate((refs[0], refs[3], refs[1], refs[2])):

            @pl.when((i ^ s) == at)
            def _(ref=ref):
                refs[-1][...] = ref[...]

    whole = pl.BlockSpec((kb, n), lambda i, s: (0, 0))
    return run(
        kernel, "in_order", [((4 * kb, n), bf16)], [side, own, far, far_pair, pair], (4,), [whole] * 4,
        [pl.BlockSpec((kb, n), lambda i, s: (i, 0))], scalars=1,
    )[0]


def weight_blocks(side, x, y, got, at, kb, dtypes):
    rows = x.shape[0]
    n = y.shape[1]

    def kernel(side_ref, x_ref, y_ref, g_ref, *outs):
        total = dot_first(x_ref[...], y_ref[...]) + g_ref[...].astype(f32)
        for q, out in enumerate(outs):

            @pl.when(pl.program_id(0) == q)
            def _(out=out):
                out[...] = total.astype(out.dtype)

    return run(
        kernel, "weight_blocks", [((kb, n), t) for t in dtypes], [side, x, y, got], (2,),
        [
            pl.BlockSpec((rows, kb), lambda i, s: (0, at + (i ^ s[0]))),
            pl.BlockSpec(y.shape, lambda i, s: (0, 0), pipeline_mode=pl.Buffered(1)),
            pl.BlockSpec((kb, n), lambda i, s: (at + (i ^ s[0]), 0)),
        ],
        [pl.BlockSpec((kb, n), lambda i, s: (0, 0))] * 2, scalars=1,
    )


def laid_out(side, terms, shape, block, axis, place):
    count = len(terms)

    def kernel(side_ref, *refs):
        out = refs[-1]

        @pl.when(pl.program_id(0) == 0)
        def _():
            place(out, [refs[4 * q][...] + refs[4 * q + 1][...].astype(f32) for q in range(count)])

        @pl.when(pl.program_id(0) == 1)
        def _():
            place(
                out, [refs[4 * q + 2][...].astype(f32) + refs[4 * q + 3][...].astype(f32) for q in range(count)]
            )

    def index(w, side_ref):
        at = w ^ side_ref[0]
        return tuple(at if a == axis else 0 for a in range(len(shape)))

    arrays = [a for t in terms for a in t]
    return run(
        kernel, "laid_out", [(shape, f32)], [side, *arrays], (2,),
        [pl.BlockSpec(a.shape, lambda w, s: (0, 0)) for a in arrays], [pl.BlockSpec(block, index)], scalars=1,
    )[0]


class Wires:
    def __init__(self, dp, tp):
        self.dp, self.tp = dp, tp
        self.order = list(range(0, dp, 2)) + list(range(1, dp, 2))
        self.far = []
        bit = 2 * PAIR
        while bit < dp:
            self.far.append(bit)
            bit *= 2

    def over_dp(self, value, mask):
        pairs = []
        for d in range(self.dp):
            for t in range(self.tp):
                pairs.append((d * self.tp + t, (d ^ mask) * self.tp + t))
        return lax.ppermute(value, AXES, pairs)

    def over_tensor(self, value, mask):
        pairs = []
        for d in range(self.dp):
            for t in range(self.tp):
                pairs.append((d * self.tp + t, d * self.tp + (t ^ mask)))
        return lax.ppermute(value, AXES, pairs)

    def to_relative(self, value, d):
        width = value.shape[1] // self.dp
        return jnp.concatenate(
            [lax.dynamic_slice_in_dim(value, (d ^ m) * width, width, 1) for m in self.order], axis=1
        )

    def to_absolute(self, value, d):
        width = value.shape[1] // self.dp
        parts = []
        for j in range(self.dp):
            m = d ^ j
            place = (m >> 1) + (self.dp // 2) * (m & 1)
            parts.append(lax.dynamic_slice_in_dim(value, place * width, width, 1))
        return jnp.concatenate(parts, axis=1)

    def groups(self):
        found = []
        for d in range(self.dp):
            if not d & PAIR:
                found.append([e * self.tp + t for e in (d, d ^ PAIR) for t in range(self.tp)])
        return found


def halves(value, side, axis):
    width = value.shape[axis] // 2
    own = lax.dynamic_slice_in_dim(value, side * width, width, axis)
    other = lax.dynamic_slice_in_dim(value, (1 - side) * width, width, axis)
    return own, other


def joined(own, other, side, axis):
    low = jnp.where(side == 0, own, other)
    high = jnp.where(side == 0, other, own)
    return jnp.concatenate([low, high], axis=axis)


class Chain:
    def __init__(self):
        self.last = ()

    def pin(self, *values):
        return lax.optimization_barrier((values, self.last))[0]

    def wait(self, *values):
        self.last = self.pin(*values)
        return self.last if len(values) > 1 else self.last[0]

    def step(self, function, *values):
        out = function(*self.pin(*values))
        self.last = out
        return out


class Piece:
    def __init__(self, wires, chain, side, own, other):
        self.wires, self.chain, self.side, self.own, self.other = wires, chain, side, own, other

    def start1(self):
        own, other = self.chain.pin(self.own, self.other)
        far = self.wires.far[0]
        self.got = [
            self.wires.over_dp(own, far), self.wires.over_dp(other, far ^ PAIR), self.wires.over_dp(other, PAIR)
        ]

    def wait1(self):
        self.got = self.chain.wait(*self.got)

    def start2(self):
        blocks = self.chain.step(in_order, self.side, self.own, *self.got)
        for bit in self.wires.far[1:]:
            blocks = jnp.concatenate([blocks, self.chain.wait(self.wires.over_dp(blocks, bit))], axis=0)
        self.blocks = blocks
        self.got = self.wires.over_dp(*self.chain.pin(blocks), NEAR)

    def wait2(self):
        self.pair = (self.blocks, self.chain.wait(self.got))


class Grad:
    def __init__(self, wires, chain, side, x, y):
        self.wires, self.chain, self.side, self.x, self.y = wires, chain, side, x, y
        self.k = x.shape[1] // 2

    def odd(self):
        self.send = self.chain.step(lambda x, y: weight_part(x, y, self.k, self.k, bf16), self.x, self.y)

    def start1(self):
        self.got = self.wires.over_dp(*self.chain.pin(self.send), NEAR)

    def wait1(self):
        self.near = self.chain.wait(self.got)

    def start2(self):
        wires, chain = self.wires, self.chain
        kb = 2 * self.k // wires.dp
        if not wires.far[1:] and kb % 128 == 0:
            blocks = lambda s, x, y, g, at, types: weight_blocks(s, x, y, g, at, kb, types)
            far, far_pair = chain.step(
                lambda s, x, y, g: blocks(s, x, y, g, 2, (bf16, bf16)), self.side, self.x, self.y, self.near
            )
            self.keep, pair = chain.step(
                lambda s, x, y, g: blocks(s, x, y, g, 0, (f32, bf16)), self.side, self.x, self.y, self.near
            )
        else:
            total = chain.step(
                lambda x, y, g: weight_part(x, y, 0, self.k, f32, g, 0), self.x, self.y, self.near
            )
            for bit in reversed(wires.far[1:]):
                rows = total.shape[0] // 2
                got = chain.wait(wires.over_dp(total[rows:].astype(bf16), bit))
                total = total[:rows] + got.astype(f32)
            at = [p ^ self.side[0] for p in (0, 1)]
            cut = lambda p: lax.dynamic_slice_in_dim(total, p * kb, kb, 0)
            self.keep, pair = cut(at[0]), cut(at[1]).astype(bf16)
            far, far_pair = cut(2 + at[0]).astype(bf16), cut(2 + at[1]).astype(bf16)
        bit = wires.far[0]
        self.got = [
            wires.over_dp(*chain.pin(far), bit),
            wires.over_dp(*chain.pin(far_pair), bit ^ PAIR),
            wires.over_dp(*chain.pin(pair), PAIR),
        ]

    def wait2(self):
        self.terms = [self.keep, *self.chain.wait(*self.got)]


class RowGather:
    def __init__(self, wires, chain, value):
        self.chain = chain
        self.got = lax.all_gather(
            *chain.pin(value), AXES, axis=0, tiled=True, axis_index_groups=wires.groups()
        )

    def wait(self):
        return self.chain.wait(self.got)


class RowSum:
    def __init__(self, wires, chain, value):
        self.chain = chain
        self.got = lax.psum_scatter(
            *chain.pin(value), AXES, scatter_dimension=0, tiled=True, axis_index_groups=wires.groups()
        )

    def wait(self):
        return self.chain.wait(self.got)


def on_device(dp, tp, hidden_in, cotangent, lengths, gain_attn, w_qkv, w_out, gain_mlp, w_gate_up, w_down):
    wires = Wires(dp, tp)
    chain = Chain()
    d = lax.axis_index("dp").astype(jnp.int32)
    t = lax.axis_index("tensor").astype(jnp.int32)
    side = (d // PAIR) % 2
    local_rows, width = hidden_in.shape
    group_rows = local_rows * tp
    kb = width // dp
    cols = w_qkv.shape[2] // 2
    head_count = cols // HEAD_DIM
    rows = Rows(wires, jnp.stack([d - PAIR * side, t, lengths[0]]), local_rows, width)

    sides = jnp.reshape(side, (1,))
    n_down, n_gu = 2, 4
    ff = w_down.shape[0] // 2
    cut, cg = ff // n_down, ff // n_gu

    def piece(own, other):
        return Piece(wires, chain, sides, own, other)

    def cut_rest(w_out, w_down, w_gate_up):
        found = [[h.T for h in halves(w_out, side, 0)]]
        whole = [h.T for h in halves(w_down, side, 0)]
        for k in range(n_down):
            found.append([h[:, k * cut : (k + 1) * cut] for h in whole])
        whole = halves(w_gate_up, side, 2)
        for k in range(n_gu):
            found.append([h[:, :, k * cg : (k + 1) * cg].reshape(kb, 2 * cg) for h in whole])
        return found

    per = n_gu // n_down
    acts, grads_gu, grads = [], [], []

    def forward_gu(k):
        act, g = chain.step(lambda *a: gated(*a, k % per), normed_second, gus[k].pair, grad_acts[k // per])
        acts.append(act)
        grads_gu.append(g)
        grads.append(Grad(wires, chain, sides, normed_second, g))

    positions = jnp.arange(group_rows, dtype=jnp.int32)
    exponent = jnp.arange(HEAD_DIM // 2).astype(f32) * (2.0 / HEAD_DIM)
    frequency = ROPE_BASE ** (-exponent)
    angles = positions.astype(f32)[:, None] * frequency[None, :]
    cosine = jnp.tile(jnp.concatenate([jnp.cos(angles), jnp.cos(angles)], axis=1), (1, head_count))
    sine = jnp.tile(jnp.concatenate([-jnp.sin(angles), jnp.sin(angles)], axis=1), (1, head_count))

    gains = jnp.stack([gain_attn, gain_mlp])[:, None]
    pair_length = wires.over_dp(lengths, PAIR)

    def ordered(mine, theirs, axis):
        return jnp.concatenate(
            [jnp.where(side == 0, mine, theirs), jnp.where(side == 0, theirs, mine)], axis=axis
        )

    got = wires.over_dp(gains, PAIR)
    gains = ordered(gains, chain.wait(got), 1)
    for bit in wires.far:
        gains = jnp.concatenate([gains, chain.wait(wires.over_dp(*chain.pin(gains), bit))], axis=1)
    w_q, w_k, w_v = (piece(*halves(w_qkv[j], side, 1)) for j in range(3))
    w_q.start1()
    gains = jnp.concatenate([gains, chain.wait(wires.over_dp(*chain.pin(gains), NEAR))], axis=1)
    gains = gains.reshape(2, width)
    input_f, scale_first, v = chain.step(rows.open_first, hidden_in, gains)
    rows_a = RowGather(wires, chain, v)
    w_o, d0, d1, g0, g1, g2, g3 = (piece(*h) for h in chain.step(cut_rest, w_out, w_down, w_gate_up))
    gus = [g0, g1, g2, g3]
    grad_rows, gv = chain.step(rows.open_cotangent, cotangent)
    table = chain.step(
        lambda a, b, *c: (ordered(a, b, 0), *c), lengths, pair_length, positions, cosine, sine
    )
    w_q.wait1()
    w_k.start1()
    w_q.start2()
    rows_g = RowGather(wires, chain, gv)
    w_k.wait1()
    w_q.wait2()
    w_v.start1()
    w_k.start2()
    normed_first = rows_a.wait()
    query_raw = chain.step(product, normed_first, w_q.pair)
    w_v.wait1()
    w_k.wait2()
    w_o.start1()
    w_v.start2()
    key_raw = chain.step(product, normed_first, w_k.pair)
    w_o.wait1()
    w_v.wait2()
    d0.start1()
    w_o.start2()
    value_raw = chain.step(product, normed_first, w_v.pair)
    saved = chain.step(lambda *a: attend(*a), *table, query_raw, key_raw, value_raw)
    attn_flat = saved[0]
    w_o.wait2()
    mixed = chain.step(lambda y, p: back([y], [p], bf16), attn_flat, w_o.pair)
    d0.wait1()
    d1.start1()
    mixed_out = RowSum(wires, chain, mixed)
    d0.start2()
    grad_half = rows_g.wait()
    d1.wait1()
    d0.wait2()
    g0.start1()
    d1.start2()
    act_0 = chain.step(product, grad_half, d0.pair)
    g0.wait1()
    d1.wait2()
    g1.start1()
    g0.start2()
    act_1 = chain.step(product, grad_half, d1.pair)
    grad_acts = [act_0, act_1]
    middle, scale_second, v = chain.step(rows.open_second, input_f, mixed_out.wait(), gains)
    g1.wait1()
    g0.wait2()
    g2.start1()
    rows_n = RowGather(wires, chain, v)
    g1.start2()
    g2.wait1()
    g1.wait2()
    g3.start1()
    g2.start2()
    normed_second = rows_n.wait()
    forward_gu(0)
    grads[0].odd()
    g3.wait1()
    g2.wait2()
    g3.start2()
    forward_gu(1)
    grads[0].start1()
    forward_gu(2)
    second = chain.step(lambda y, p: back(y, p, f32), grads_gu, [g.pair for g in gus[:3]])
    g3.wait2()
    forward_gu(3)
    second = chain.step(lambda y, p, s: back([y], [p], bf16, s), grads_gu[3], g3.pair, second)
    grads[1].odd()
    grads[0].wait1()
    sum_second = RowSum(wires, chain, second)
    grads[1].start1()
    grads[0].start2()
    grads[2].odd()
    acts = [jnp.concatenate(acts[k * per : (k + 1) * per], axis=1) for k in range(n_down)]
    grads += [Grad(wires, chain, sides, grad_half, a) for a in acts]
    grads[3].odd()
    grads[1].wait1()
    grads[0].wait2()
    grads[2].start1()
    grads[1].start2()
    mlp_part = chain.step(lambda y, p: back(y, p, bf16), acts, [d0.pair, d1.pair])
    grads[4].odd()
    grads[2].wait1()
    grads[1].wait2()
    part_gain_mlp, grad_middle, v = chain.step(
        rows.close_second, sum_second.wait(), gains, middle, scale_second, grad_rows
    )
    rows_m = RowGather(wires, chain, v)
    grads[3].start1()
    grads[2].start2()
    grads[5].odd()
    grads[3].wait1()
    grads[2].wait2()
    grads[4].start1()
    grads[3].start2()
    grads[4].wait1()
    grads[3].wait2()
    grads[5].start1()
    mlp = RowSum(wires, chain, mlp_part)
    grads[4].start2()
    middle_half = rows_m.wait()
    grads.append(Grad(wires, chain, sides, middle_half, attn_flat))
    grads[6].odd()
    grad_mixed = chain.step(lambda x, p: product(x, p, bf16), middle_half, w_o.pair)
    grads[5].wait1()
    grads[4].wait2()
    grads[6].start1()
    grads[5].start2()
    grad_proj = chain.step(lambda *a: attend_back(*a), *table, saved, grad_mixed)
    grads += [Grad(wires, chain, sides, normed_first, g) for g in grad_proj]
    grads[7].odd()
    first = chain.step(
        lambda y, p: back(y, p, bf16), grad_proj, [w_q.pair, w_k.pair, w_v.pair]
    )
    grads[6].wait1()
    grads[5].wait2()
    grads[7].start1()
    sum_first = RowSum(wires, chain, first)
    grads[6].start2()
    grads[8].odd()
    grads[9].odd()

    def gain_open(part):
        total = jnp.concatenate([part, part_gain_mlp]).reshape(2, dp, kb)
        mine, theirs = total[:, 0::2], total[:, 1::2]
        low = jnp.where(side == 0, mine, theirs)
        high = jnp.where(side == 0, theirs, mine)
        return jnp.stack([low, high], axis=2).reshape(2, dp, kb)

    def gain_start(bit):
        nonlocal total, got
        rows = total.shape[1] // 2
        got = wires.over_dp(*chain.pin(total[:, rows:]), bit)
        total = total[:, :rows]

    def gain_wait():
        nonlocal total
        total = total + chain.wait(got)

    def place_gu(ref, parts):
        for k, p in enumerate(parts):
            ref[:, 0, k * cg : (k + 1) * cg] = p[:, :cg]
            ref[:, 1, k * cg : (k + 1) * cg] = p[:, cg:]

    def place_rows(ref, parts):
        n = parts[0].shape[1]
        for k, p in enumerate(parts):
            ref[k * n : (k + 1) * n] = p.T

    def place_stack(ref, parts):
        for k, p in enumerate(parts):
            ref[k] = p

    def lay(which, shape, axis, place):
        block = tuple(n // 2 if a == axis else n for a, n in enumerate(shape))
        return chain.step(
            lambda t: laid_out(sides, t, shape, block, axis, place), [grads[i].terms for i in which]
        )

    grads[7].wait1()
    grads[6].wait2()
    grads[8].start1()
    grads[7].start2()
    layer_out = chain.step(rows.close_layer, mlp.wait(), middle)
    grad_gate_up = lay((0, 1, 2, 3), (kb, 2, 2 * ff), 2, place_gu)
    grads[8].wait1()
    grads[7].wait2()
    grads[9].start1()
    grads[8].start2()
    grad_down = lay((4, 5), (2 * ff, kb), 0, place_rows)
    grad_out = lay((6,), (2 * cols, kb), 0, place_rows)
    grads[9].wait1()
    grads[8].wait2()
    grads[9].start2()
    part_gain_attn, grad_in = chain.step(
        rows.close_first, sum_first.wait(), gains, input_f, scale_first, grad_middle
    )
    total = gain_open(part_gain_attn)
    for bit in [NEAR] + wires.far[::-1] + [PAIR]:
        gain_start(bit)
        gain_wait()
    total = total[:, 0]
    total = total + chain.wait(wires.over_tensor(*chain.pin(total), 1))
    total = total + chain.wait(wires.over_tensor(*chain.pin(total), 2))
    grads[9].wait2()
    grad_qkv = lay((7, 8, 9), (3, kb, 2 * cols), 2, place_stack)
    return (layer_out, grad_in, total[0], grad_qkv, grad_out, total[1], grad_gate_up, grad_down)


def solution(mesh):
    placed = (
        P(("dp", "tensor"), None),
        P(("dp", "tensor"), None),
        P("dp"),
        P("dp"),
        P(None, "dp", "tensor"),
        P("tensor", "dp"),
        P("dp"),
        P("dp", None, "tensor"),
        P("tensor", "dp"),
    )
    dp, tp = mesh.shape["dp"], mesh.shape["tensor"]

    def body(*args):
        return on_device(dp, tp, *args)

    return jax.shard_map(
        body,
        mesh=mesh,
        in_specs=placed,
        out_specs=(
            P(("dp", "tensor"), None),
            P(("dp", "tensor"), None),
            P("dp"),
            P(None, "dp", "tensor"),
            P("tensor", "dp"),
            P("dp"),
            P("dp", None, "tensor"),
            P("tensor", "dp"),
        ),
        check_vma=False,
    )
```

```python
import math

import jax
import jax.numpy as jnp
from jax import lax
from jax.experimental import pallas as pl
from jax.experimental.pallas import tpu as pltpu
from jax.sharding import PartitionSpec as P

HEAD_DIM = 96
NORM_EPS = 1e-05
ROPE_BASE = 10000.0
AXES = ("dp", "tensor")
PAIR = 2
NEAR = 1
NEGATIVE = -1e30

bf16 = jnp.bfloat16
f32 = jnp.float32


def dot_last(a, b):
    return lax.dot_general(a, b, (((1,), (1,)), ((), ())), preferred_element_type=f32)


def dot_first(a, b):
    return lax.dot_general(a, b, (((0,), (0,)), ((), ())), preferred_element_type=f32)


def turned(u, low):
    width = u.shape[1]
    half = HEAD_DIM // 2
    return jnp.where(low, pltpu.roll(u, width - half, 1), pltpu.roll(u, half, 1))


def low_lanes(shape):
    lane = lax.broadcasted_iota(jnp.int32, shape, 1)
    low = lane < 0
    for h in range(shape[1] // HEAD_DIM):
        low = low | ((lane >= h * HEAD_DIM) & (lane < h * HEAD_DIM + HEAD_DIM // 2))
    return low


def group_block(ref):
    return ref[...]


def put_block(ref, v):
    ref[...] = v


def masked_scores(qh, kh, allowed):
    return jnp.where(allowed, dot_last(qh, kh) * (1.0 / math.sqrt(HEAD_DIM)), NEGATIVE)


def allowed_pairs(rows_ref, cols_ref, length):
    rp, cp = rows_ref[...], cols_ref[...]
    return (cp <= rp) & ((rp < length) == (cp < length))


def attend_kernel(len_ref, rows_ref, cols_ref, cos_ref, sin_ref, q_ref, k_ref, v_ref,
                  o_ref, qo_ref, ko_ref, vo_ref, lse_ref):
    allowed = allowed_pairs(rows_ref, cols_ref, len_ref[pl.program_id(0)])
    q, k = group_block(q_ref), group_block(k_ref)
    cosine, sine = (jnp.concatenate([r[...]] * (q.shape[1] // HEAD_DIM), axis=1) for r in (cos_ref, sin_ref))
    low = low_lanes(cosine.shape)
    q = q * cosine + turned(q, low) * sine
    k = k * cosine + turned(k, low) * sine
    v = group_block(v_ref)
    put_block(qo_ref, q.astype(bf16))
    put_block(ko_ref, k.astype(bf16))
    put_block(vo_ref, v.astype(bf16))
    outs, totals = [], []
    for h in range(q.shape[1] // HEAD_DIM):
        c = slice(h * HEAD_DIM, (h + 1) * HEAD_DIM)
        s = masked_scores(q[:, c].astype(bf16), k[:, c].astype(bf16), allowed)
        top = jnp.max(s, axis=1, keepdims=True)
        e = jnp.exp(s - top)
        total = jnp.sum(e, axis=1, keepdims=True)
        prob = (e * (1.0 / total)).astype(bf16)
        outs.append(jnp.dot(prob, v[:, c].astype(bf16), preferred_element_type=f32))
        totals.append(top + jnp.log(total))
    put_block(o_ref, jnp.concatenate(outs, axis=1).astype(bf16))
    put_block(lse_ref, jnp.concatenate(totals, axis=1))


def attend_back_kernel(len_ref, rows_ref, cols_ref, cos_ref, sin_ref, q_ref, k_ref, v_ref, o_ref, g_ref, lse_ref,
                       dq_ref, dk_ref, dv_ref):
    allowed = allowed_pairs(rows_ref, cols_ref, len_ref[pl.program_id(0)])
    q, k, v, g = (group_block(r).astype(f32) for r in (q_ref, k_ref, v_ref, g_ref))
    go = g * group_block(o_ref).astype(f32)
    totals = group_block(lse_ref)
    dqs, dks, dvs = [], [], []
    for h in range(q.shape[1] // HEAD_DIM):
        c = slice(h * HEAD_DIM, (h + 1) * HEAD_DIM)
        qh, kh, vh, gh = (u[:, c].astype(bf16) for u in (q, k, v, g))
        delta = jnp.sum(go[:, c], axis=1, keepdims=True)
        prob = jnp.exp(masked_scores(qh, kh, allowed) - totals[:, h : h + 1])
        ds = (prob * (dot_last(gh, vh) - delta) * (1.0 / math.sqrt(HEAD_DIM))).astype(bf16)
        dqs.append(jnp.dot(ds, kh, preferred_element_type=f32))
        dks.append(dot_first(ds, qh))
        dvs.append(dot_first(prob.astype(bf16), gh))
    cosine, sine = (jnp.concatenate([r[...]] * (q.shape[1] // HEAD_DIM), axis=1) for r in (cos_ref, sin_ref))
    low = low_lanes(cosine.shape)
    for ref, parts in ((dq_ref, dqs), (dk_ref, dks)):
        u = jnp.concatenate(parts, axis=1)
        put_block(ref, (u * cosine - turned(u, low) * sine).astype(bf16))
    put_block(dv_ref, jnp.concatenate(dvs, axis=1).astype(bf16))


def attend_specs(group_rows, cols, lanes):
    tall = pl.BlockSpec((group_rows, cols), lambda g: (g, 0))
    table = pl.BlockSpec((group_rows, HEAD_DIM), lambda g: (g, 0))
    head = [
        pl.BlockSpec(memory_space=pltpu.SMEM),
        pl.BlockSpec((group_rows, 1), lambda g: (g, 0)),
        pl.BlockSpec((1, group_rows), lambda g: (0, g)),
        table,
        table,
    ]
    return head, tall, pl.BlockSpec((group_rows, lanes), lambda g: (g, 0))


def attend(lengths, positions, cosine, sine, q, k, v):
    rows, cols = q.shape
    lanes = cols // HEAD_DIM
    head, tall, thin = attend_specs(rows // 2, cols, lanes)
    return run(
        attend_kernel, "attend", [((rows, cols), bf16)] * 4 + [((rows, lanes), f32)],
        [lengths, positions[:, None], positions[None, :], cosine, sine, q, k, v], (2,),
        head + [tall] * 3, [tall] * 4 + [thin],
    )


def attend_back(lengths, positions, cosine, sine, saved, g):
    o, q, k, v, lse = saved
    rows, cols = q.shape
    head, tall, thin = attend_specs(rows // 2, cols, cols // HEAD_DIM)
    return run(
        attend_back_kernel, "attend_back", [((rows, cols), bf16)] * 3,
        [lengths, positions[:, None], positions[None, :], cosine, sine, q, k, v, o, g, lse], (2,),
        head + [tall] * 5 + [thin], [tall] * 3,
    )


def run(kernel, name, outs, args, grid=(), in_specs=None, out_specs=None, scratch=(), scalars=0):
    whole = pl.BlockSpec(memory_space=pltpu.VMEM)
    if in_specs is None:
        in_specs = [whole] * (len(args) - scalars)
    if out_specs is None:
        out_specs = [whole] * len(outs)
    got = pl.pallas_call(
        kernel,
        out_shape=[jax.ShapeDtypeStruct(s, t) for s, t in outs],
        grid_spec=pltpu.PrefetchScalarGridSpec(
            num_scalar_prefetch=scalars, grid=grid, in_specs=in_specs, out_specs=out_specs, scratch_shapes=scratch
        ),
        compiler_params=pltpu.CompilerParams(vmem_limit_bytes=52 << 20),
        cost_estimate=pl.CostEstimate(flops=1, bytes_accessed=1, transcendentals=0),
        name=name,
    )(*args)
    return list(got)


SMALL = pl.BlockSpec(memory_space=pltpu.SMEM)
VMEM = pl.BlockSpec(memory_space=pltpu.VMEM)


def tiles(rows, width):
    return pl.BlockSpec((rows, width), lambda i: (i, 0))


def still(shape):
    return pl.BlockSpec(shape, lambda i: (0,) * len(shape), pipeline_mode=pl.Buffered(1))


def product(x, pair, dtype=f32):
    rows, width = x.shape
    k, n = pair[0].shape
    tile = rows // 4

    def kernel(x_ref, even, odd, out):
        total = jnp.dot(x_ref[:, :k], even[...], preferred_element_type=f32)
        total += jnp.dot(x_ref[:, k:], odd[...], preferred_element_type=f32)
        out[...] = total.astype(dtype)

    return run(
        kernel, "product", [((rows, n), dtype)], [x, *pair], (4,),
        [tiles(tile, width)] + [still((k, n))] * 2, [tiles(tile, n)],
    )[0]


def gated(x, pair, grad_act, column):
    rows, width = x.shape
    k, n = pair[0].shape
    c = n // 2
    tile = rows // 4

    def kernel(x_ref, even, odd, ga_ref, act, grad):
        total = jnp.dot(x_ref[:, :k], even[...], preferred_element_type=f32)
        total += jnp.dot(x_ref[:, k:], odd[...], preferred_element_type=f32)
        gate, up, ga = total[:, :c], total[:, c:], ga_ref[...]
        sig = jax.nn.sigmoid(gate)
        act[...] = (gate * sig * up).astype(bf16)
        grad[:, :c] = (ga * up * sig * (1.0 + gate * (1.0 - sig))).astype(bf16)
        grad[:, c:] = (ga * gate * sig).astype(bf16)

    return run(
        kernel, "gated", [((rows, c), bf16), ((rows, n), bf16)], [x, *pair, grad_act], (4,),
        [tiles(tile, width)] + [still((k, n))] * 2 + [pl.BlockSpec((tile, c), lambda i: (i, column))],
        [tiles(tile, c), tiles(tile, n)],
    )


def back(ys, pairs, dtype, part=None, turn=True, normed=None):
    rows = ys[0].shape[0]
    k = pairs[0][0].shape[0]
    count = len(ys)
    tile = rows // 4
    extra = [a for a in (part, normed) if a is not None]
    more = len(extra)

    def kernel(*refs):
        y_refs, w_refs, out = refs[:count], refs[count : 3 * count], refs[3 * count + more]
        for s in range(2):
            c = slice(s * k, (s + 1) * k)
            total = refs[3 * count][:, c] if part is not None else None
            for y, w in zip(y_refs, w_refs[s::2]):
                term = dot_last(y[...], w[...])
                total = term if total is None else total + term
            if normed is not None:
                sums = jnp.sum(total * refs[3 * count][:, c].astype(f32), axis=0, keepdims=True)

                @pl.when(pl.program_id(0) == 0)
                def _():
                    refs[-1][:, c] = sums

                @pl.when(pl.program_id(0) > 0)
                def _():
                    refs[-1][:, c] += sums

            total = total.astype(dtype)
            if not turn:
                out[:, c] = total
                continue

            i = pl.program_id(0)
            swapped = (i == 1) | (i == 2)

            @pl.when(jnp.logical_not(swapped))
            def _():
                out[:, c] = total

            @pl.when(swapped)
            def _():
                out[: tile // 2, c] = total[tile // 2 :]
                out[tile // 2 :, c] = total[: tile // 2]

    flat = [w for p in pairs for w in p]
    outs = [((rows, 2 * k), dtype)] + ([] if normed is None else [((1, 2 * k), f32)])
    got = run(
        kernel, "back", outs, [*ys, *flat, *extra], (4,),
        [tiles(tile, y.shape[1]) for y in ys] + [still(w.shape) for w in flat] + [tiles(tile, 2 * k)] * more,
        [
            pl.BlockSpec((tile, 2 * k), lambda i: (jnp.where(i < 2, i, 5 - i) if turn else i, 0)),
            pl.BlockSpec((1, 2 * k), lambda i: (0, 0)),
        ][: len(outs)],
    )
    return got[0] if normed is None else got


def side_by_side(side, mine, theirs):
    rows, n = mine.shape

    def kernel(side_ref, a, b, out):
        for q, ref in enumerate((a, b)):

            @pl.when(pl.program_id(0) == q)
            def _(ref=ref):
                out[...] = ref[...].reshape(1, rows, n)

    whole = pl.BlockSpec((rows, n), lambda i, s: (0, 0))
    return run(
        kernel, "side_by_side", [((2, rows, n), bf16)], [side, mine, theirs], (2,), [whole] * 2,
        [pl.BlockSpec((1, rows, n), lambda i, s: (i ^ s[0], 0, 0))], scalars=1,
    )[0]


def weight_part(x, y, first, count, dtype):
    rows = x.shape[0]
    n = y.shape[1]
    tile = count if count <= 768 else count // 2
    base = first // tile

    def kernel(x_ref, y_ref, out):
        out[...] = dot_first(x_ref[...], y_ref[...]).astype(dtype)

    return run(
        kernel, "weight_part", [((count, n), dtype)], [x, y], (count // tile,),
        [pl.BlockSpec((rows, tile), lambda i: (0, i + base)), still(y.shape)], [tiles(tile, n)],
    )[0]


class Rows:
    def __init__(self, wires, info, rows, width):
        self.wires, self.info, self.rows, self.width = wires, info, rows, width
        self.kb = width // wires.dp
        self.inside = self.kb % 128 == 0

    def load_relative(self, ref, info):
        if not self.inside:
            return ref[...].astype(f32)
        kb = self.kb
        parts = []
        for m in self.wires.order:
            parts.append(ref[:, pl.ds(pl.multiple_of((info[0] ^ m) * kb, 128), kb)].astype(f32))
        return jnp.concatenate(parts, axis=1)

    def store_absolute(self, ref, value, scratch, info):
        if not self.inside:
            ref[...] = value
            return
        kb, half = self.kb, self.wires.dp // 2
        scratch[...] = value
        for j in range(self.wires.dp):
            m = info[0] ^ j
            place = (m >> 1) + half * (m & 1)
            ref[:, j * kb : (j + 1) * kb] = scratch[:, pl.ds(pl.multiple_of(place * kb, 128), kb)]

    def relative(self, x):
        return x if self.inside else self.wires.to_relative(x, self.info[0])

    def absolute(self, x):
        return x if self.inside else self.wires.to_absolute(x, self.info[0])

    def live(self, info, shape):
        row = info[1] * shape[0] + lax.broadcasted_iota(jnp.int32, (shape[0], 1), 0)
        return (row < info[2]).astype(f32)

    def outs(self, *dtypes):
        return [((self.rows, self.width), t) for t in dtypes]

    def open_first(self, x, gains):
        def kernel(info, x_ref, gain_ref, rel, scale_ref, v):
            x = self.load_relative(x_ref, info)
            scale = lax.rsqrt(jnp.mean(x * x, axis=1, keepdims=True) + NORM_EPS)
            rel[...] = x
            scale_ref[...] = scale
            v[...] = (x * scale * gain_ref[0:1].astype(f32)).astype(bf16)

        return run(
            kernel, "open_first", self.outs(f32) + [((self.rows, 1), f32)] + self.outs(bf16),
            [self.info, self.relative(x), gains], in_specs=[SMALL, VMEM, VMEM],
        )

    def open_cotangent(self, c):
        def kernel(info, c_ref, g, v):
            x = self.load_relative(c_ref, info)
            x = x * self.live(info, x.shape)
            g[...] = x
            v[...] = x.astype(bf16)

        return run(
            kernel, "open_cotangent", self.outs(f32, bf16), [self.info, self.relative(c)], in_specs=[SMALL, VMEM]
        )

    def open_second(self, x, got, gains):
        def kernel(x_ref, got_ref, gain_ref, mid, scale_ref, v):
            middle = x_ref[...] + got_ref[...].astype(f32)
            scale = lax.rsqrt(jnp.mean(middle * middle, axis=1, keepdims=True) + NORM_EPS)
            mid[...] = middle
            scale_ref[...] = scale
            v[...] = (middle * scale * gain_ref[1:2].astype(f32)).astype(bf16)

        return run(
            kernel, "open_second", self.outs(f32) + [((self.rows, 1), f32)] + self.outs(bf16), [x, got, gains]
        )

    def norm_back(self, got_ref, gain, x_ref, scale_ref, rows_ref, part=None):
        grad = got_ref[...].astype(f32)
        scale = scale_ref[...]
        unit = x_ref[...] * scale
        if part is not None:
            part[...] = jnp.sum(grad * unit, axis=0, keepdims=True)
        e = grad * gain
        return rows_ref[...] + scale * (e - unit * jnp.mean(e * unit, axis=1, keepdims=True))

    def close_second(self, got, gains, middle, scale, rows):
        def kernel(got_ref, gain_ref, x_ref, scale_ref, rows_ref, part, mid, v):
            grad = self.norm_back(got_ref, gain_ref[1:2].astype(f32), x_ref, scale_ref, rows_ref, part)
            mid[...] = grad
            v[...] = grad.astype(bf16)

        return run(
            kernel, "close_second", [((1, self.width), f32)] + self.outs(f32, bf16),
            [got, gains, middle, scale, rows],
        )

    def close_first(self, got, gains, x, scale, rows):
        def kernel(info, got_ref, gain_ref, x_ref, scale_ref, rows_ref, out, scratch):
            grad = self.norm_back(got_ref, gain_ref[0:1].astype(f32), x_ref, scale_ref, rows_ref)
            self.store_absolute(out, grad, scratch, info)

        out, = run(
            kernel, "close_first", self.outs(f32),
            [self.info, got, gains, x, scale, rows], in_specs=[SMALL] + [VMEM] * 5,
            scratch=[pltpu.VMEM((self.rows, self.width), f32)],
        )
        return self.absolute(out)

    def close_layer(self, got, middle):
        def kernel(info, got_ref, mid_ref, out, scratch):
            total = mid_ref[...] + got_ref[...].astype(f32)
            self.store_absolute(out, total * self.live(info, total.shape), scratch, info)

        out, = run(
            kernel, "close_layer", self.outs(f32), [self.info, got, middle], in_specs=[SMALL] + [VMEM] * 2,
            scratch=[pltpu.VMEM((self.rows, self.width), f32)],
        )
        return self.absolute(out)


def in_order(side, own, far, far_pair, pair):
    kb, n = own.shape

    def kernel(side_ref, *refs):
        i, s = pl.program_id(0), side_ref[0]
        for at, ref in enumerate((refs[0], refs[3], refs[1], refs[2])):

            @pl.when((i ^ s) == at)
            def _(ref=ref):
                refs[-1][...] = ref[...]

    whole = pl.BlockSpec((kb, n), lambda i, s: (0, 0))
    return run(
        kernel, "in_order", [((4 * kb, n), bf16)], [side, own, far, far_pair, pair], (4,), [whole] * 4,
        [pl.BlockSpec((kb, n), lambda i, s: (i, 0))], scalars=1,
    )[0]


def added(side, keep, got, at, kb, dtypes):
    n = keep.shape[1]

    def kernel(side_ref, k0, g0, k1, g1, first, second):
        first[...] = (k0[...] + g0[...].astype(f32)).astype(first.dtype)
        second[...] = (k1[...] + g1[...].astype(f32)).astype(second.dtype)

    block = lambda q: pl.BlockSpec((kb, n), lambda i, s: (at + (q ^ s[0]), 0))
    whole = pl.BlockSpec((kb, n), lambda i, s: (0, 0))
    return run(
        kernel, "added", [((kb, n), t) for t in dtypes], [side, keep, got, keep, got], (1,),
        [block(0), block(0), block(1), block(1)], [whole, whole], scalars=1,
    )


def cut_gate_up(side, w, count):
    kb, _, width = w.shape
    c = width // 2 // count

    def kernel(side_ref, w_ref, *outs):
        for k, out in enumerate(outs):
            out[:, :c] = w_ref[:, 0, k * c : (k + 1) * c]
            out[:, c:] = w_ref[:, 1, k * c : (k + 1) * c]

    return run(
        kernel, "cut_gate_up", [((kb, 2 * c), bf16)] * count, [side, w], (1,),
        [pl.BlockSpec((kb, 2, width // 2), lambda i, s: (0, 0, s[0]))],
        [pl.BlockSpec((kb, 2 * c), lambda i, s: (0, 0))] * count, scalars=1,
    )


def cut_rows(side, w, count):
    rows, kb = w.shape
    c = rows // 2 // count

    def kernel(side_ref, w_ref, *outs):
        for k, out in enumerate(outs):
            out[...] = w_ref[k * c : (k + 1) * c].T

    return run(
        kernel, "cut_rows", [((kb, c), bf16)] * count, [side, w], (1,),
        [pl.BlockSpec((rows // 2, kb), lambda i, s: (s[0], 0))],
        [pl.BlockSpec((kb, c), lambda i, s: (0, 0))] * count, scalars=1,
    )


def cut_columns(side, w):
    count, kb, width = w.shape

    def kernel(side_ref, w_ref, *outs):
        for k, out in enumerate(outs):
            out[...] = w_ref[k]

    return run(
        kernel, "cut_columns", [((kb, width // 2), bf16)] * count, [side, w], (1,),
        [pl.BlockSpec((count, kb, width // 2), lambda i, s: (0, 0, s[0]))],
        [pl.BlockSpec((kb, width // 2), lambda i, s: (0, 0))] * count, scalars=1,
    )


def laid_out(side, terms, shape, block, axis, place):
    count = len(terms)

    def kernel(side_ref, *refs):
        out = refs[-1]

        @pl.when(pl.program_id(0) == 0)
        def _():
            place(out, [refs[4 * q][...] + refs[4 * q + 1][...].astype(f32) for q in range(count)])

        @pl.when(pl.program_id(0) == 1)
        def _():
            place(
                out, [refs[4 * q + 2][...].astype(f32) + refs[4 * q + 3][...].astype(f32) for q in range(count)]
            )

    def index(w, side_ref):
        at = w ^ side_ref[0]
        return tuple(at if a == axis else 0 for a in range(len(shape)))

    arrays = [a for t in terms for a in t]
    return run(
        kernel, "laid_out", [(shape, f32)], [side, *arrays], (2,),
        [pl.BlockSpec(a.shape, lambda w, s: (0, 0)) for a in arrays], [pl.BlockSpec(block, index)], scalars=1,
    )[0]


class Wires:
    def __init__(self, dp, tp):
        self.dp, self.tp = dp, tp
        self.order = list(range(0, dp, 2)) + list(range(1, dp, 2))
        self.far = []
        bit = 2 * PAIR
        while bit < dp:
            self.far.append(bit)
            bit *= 2

    def over_dp(self, value, mask):
        pairs = []
        for d in range(self.dp):
            for t in range(self.tp):
                pairs.append((d * self.tp + t, (d ^ mask) * self.tp + t))
        return lax.ppermute(value, AXES, pairs)

    def over_tensor(self, value, mask):
        pairs = []
        for d in range(self.dp):
            for t in range(self.tp):
                pairs.append((d * self.tp + t, d * self.tp + (t ^ mask)))
        return lax.ppermute(value, AXES, pairs)

    def to_relative(self, value, d):
        width = value.shape[1] // self.dp
        return jnp.concatenate(
            [lax.dynamic_slice_in_dim(value, (d ^ m) * width, width, 1) for m in self.order], axis=1
        )

    def to_absolute(self, value, d):
        width = value.shape[1] // self.dp
        parts = []
        for j in range(self.dp):
            m = d ^ j
            place = (m >> 1) + (self.dp // 2) * (m & 1)
            parts.append(lax.dynamic_slice_in_dim(value, place * width, width, 1))
        return jnp.concatenate(parts, axis=1)

    def walk(self):
        return [t ^ (t >> 1) for t in range(self.tp)]

    def pairs(self, walk):
        there = self.walk() if walk else list(range(self.tp))
        back = there[::-1] if walk else there
        return [
            [d * self.tp + t for t in there] + [(d ^ PAIR) * self.tp + t for t in back]
            for d in range(self.dp)
            if not d & PAIR
        ]

    def singles(self):
        return [[d * self.tp + t for t in range(self.tp)] for d in range(self.dp)]


def halves(value, side, axis):
    width = value.shape[axis] // 2
    own = lax.dynamic_slice_in_dim(value, side * width, width, axis)
    other = lax.dynamic_slice_in_dim(value, (1 - side) * width, width, axis)
    return own, other


def joined(own, other, side, axis):
    low = jnp.where(side == 0, own, other)
    high = jnp.where(side == 0, other, own)
    return jnp.concatenate([low, high], axis=axis)


class Chain:
    def __init__(self):
        self.last = ()

    def pin(self, *values):
        return lax.optimization_barrier((values, self.last))[0]

    def wait(self, *values):
        self.last = self.pin(*values)
        return self.last if len(values) > 1 else self.last[0]

    def step(self, function, *values):
        out = function(*self.pin(*values))
        self.last = out
        return out


class Piece:
    def __init__(self, wires, chain, side, own, other):
        self.wires, self.chain, self.side, self.own, self.other = wires, chain, side, own, other

    def start1(self):
        own, other = self.chain.pin(self.own, self.other)
        far = self.wires.far[0]
        self.got = [
            self.wires.over_dp(own, far), self.wires.over_dp(other, far ^ PAIR), self.wires.over_dp(other, PAIR)
        ]

    def wait1(self):
        self.got = self.chain.wait(*self.got)

    def start2(self):
        blocks = self.chain.step(in_order, self.side, self.own, *self.got)
        for bit in self.wires.far[1:]:
            blocks = jnp.concatenate([blocks, self.chain.wait(self.wires.over_dp(blocks, bit))], axis=0)
        self.blocks = blocks
        self.got = self.wires.over_dp(*self.chain.pin(blocks), NEAR)

    def wait2(self):
        self.pair = (self.blocks, self.chain.wait(self.got))


class Grad:
    def __init__(self, wires, chain, side, x, y):
        self.wires, self.chain, self.side, self.x, self.y = wires, chain, side, x, y
        self.k = x.shape[1] // 2

    def odd(self):
        self.send = self.chain.step(lambda x, y: weight_part(x, y, self.k, self.k, bf16), self.x, self.y)

    def start1(self):
        self.got = self.wires.over_dp(*self.chain.pin(self.send), NEAR)

    def wait1(self):
        self.near = self.chain.wait(self.got)

    def even(self):
        self.ahead = self.chain.step(lambda x, y: weight_part(x, y, 0, self.k, f32), self.x, self.y)

    def add(self):
        wires, chain = self.wires, self.chain
        kb = 2 * self.k // wires.dp
        if not wires.far[1:]:
            self.sends = chain.step(
                lambda s, e, g: added(s, e, g, 2, kb, (bf16, bf16)), self.side, self.ahead, self.near
            )
            self.keep, pair = chain.step(
                lambda s, e, g: added(s, e, g, 0, kb, (f32, bf16)), self.side, self.ahead, self.near
            )
            self.sends = [*self.sends, pair]
            return
        total = self.ahead + self.near.astype(f32)
        for b in reversed(wires.far[1:]):
            rows = total.shape[0] // 2
            got = chain.wait(wires.over_dp(total[rows:].astype(bf16), b))
            total = total[:rows] + got.astype(f32)
        cut = lambda p: lax.dynamic_slice_in_dim(total, (p ^ self.side[0]) * kb, kb, 0)
        far = lambda p: lax.dynamic_slice_in_dim(total, (2 + (p ^ self.side[0])) * kb, kb, 0)
        self.keep = cut(0)
        self.sends = [far(0).astype(bf16), far(1).astype(bf16), cut(1).astype(bf16)]

    def start2(self):
        bit = self.wires.far[0]
        sends = self.chain.pin(*self.sends)
        self.got = [self.wires.over_dp(v, m) for v, m in zip(sends, (bit, bit ^ PAIR, PAIR))]

    def wait_pair(self):
        self.got[2] = self.chain.wait(self.got[2])

    def wait2(self):
        self.terms = [self.keep, *self.chain.wait(*self.got)]


class RowGather:
    def __init__(self, wires, chain, value):
        self.chain = chain
        self.got = lax.all_gather(
            *chain.pin(value), AXES, axis=0, tiled=True, axis_index_groups=wires.pairs(False)
        )

    def wait(self):
        return self.chain.wait(self.got)


class PairGather:
    def __init__(self, wires, chain, side, value):
        self.wires, self.chain, self.side, self.value = wires, chain, side, value
        self.got = wires.over_dp(*chain.pin(value), PAIR)

    def wait1(self):
        self.both = self.chain.step(side_by_side, self.side, self.value, self.chain.wait(self.got))

    def start2(self):
        got = lax.all_gather(
            *self.chain.pin(self.both), AXES, axis=1, tiled=True, axis_index_groups=self.wires.singles()
        )
        self.got = got.reshape(-1, got.shape[2])

    def wait(self):
        return self.chain.wait(self.got)


class RowSum:
    def __init__(self, wires, chain, value):
        self.chain = chain
        self.got = lax.psum_scatter(
            *chain.pin(value), AXES, scatter_dimension=0, tiled=True, axis_index_groups=wires.pairs(True)
        )

    def wait(self):
        return self.chain.wait(self.got)


def on_device(dp, tp, hidden_in, cotangent, lengths, gain_attn, w_qkv, w_out, gain_mlp, w_gate_up, w_down):
    wires = Wires(dp, tp)
    chain = Chain()
    d = lax.axis_index("dp").astype(jnp.int32)
    t = lax.axis_index("tensor").astype(jnp.int32)
    side = (d // PAIR) % 2
    local_rows, width = hidden_in.shape
    group_rows = local_rows * tp
    kb = width // dp
    cols = w_qkv.shape[2] // 2
    rows = Rows(wires, jnp.stack([d - PAIR * side, t, lengths[0]]), local_rows, width)

    sides = jnp.reshape(side, (1,))
    n_down, n_gu = 2, 4
    ff = w_down.shape[0] // 2
    cut, cg = ff // n_down, ff // n_gu

    def piece(own, other):
        return Piece(wires, chain, sides, own, other)

    def both(cut, w, *count):
        return list(zip(*(cut(s, w, *count) for s in (sides, 1 - sides))))

    per = n_gu // n_down
    acts, grads_gu, grads = [], [], []

    def forward_gu(k):
        act, g = chain.step(lambda *a: gated(*a, k % per), normed_second, gus[k].pair, grad_acts[k // per])
        acts.append(act)
        grads_gu.append(g)
        grads.append(Grad(wires, chain, sides, normed_second, g))

    positions = jnp.tile(jnp.arange(group_rows, dtype=jnp.int32), 2)
    exponent = jnp.arange(HEAD_DIM // 2).astype(f32) * (2.0 / HEAD_DIM)
    frequency = ROPE_BASE ** (-exponent)
    angles = positions.astype(f32)[:, None] * frequency[None, :]
    cosine = jnp.concatenate([jnp.cos(angles), jnp.cos(angles)], axis=1)
    sine = jnp.concatenate([-jnp.sin(angles), jnp.sin(angles)], axis=1)

    gains = jnp.stack([gain_attn, gain_mlp])[:, None]
    pair_length = wires.over_dp(lengths, PAIR)

    def ordered(mine, theirs, axis):
        return jnp.concatenate(
            [jnp.where(side == 0, mine, theirs), jnp.where(side == 0, theirs, mine)], axis=axis
        )

    masks = [PAIR, wires.far[0], wires.far[0] ^ PAIR]
    got = [wires.over_dp(gains, m) for m in masks]
    grad_rows, gv = chain.step(rows.open_cotangent, cotangent)
    got = chain.wait(*got)
    rows_g = PairGather(wires, chain, sides, gv)
    w_q, w_k, w_v = (piece(*h) for h in both(cut_columns, w_qkv))
    gains = jnp.concatenate([ordered(gains, got[0], 1), ordered(got[1], got[2], 1)], axis=1)
    for bit in wires.far[1:]:
        gains = jnp.concatenate([gains, chain.wait(wires.over_dp(*chain.pin(gains), bit))], axis=1)
    gains = jnp.concatenate([gains, chain.wait(wires.over_dp(*chain.pin(gains), NEAR))], axis=1)
    gains = gains.reshape(2, width)
    input_f, scale_first, v = chain.step(rows.open_first, hidden_in, gains)
    rows_g.wait1()
    rows_a = RowGather(wires, chain, v)
    w_q.start1()
    table = chain.step(
        lambda a, b, *c: (ordered(a, b, 0), *c), lengths, pair_length, positions, cosine, sine
    )
    w_q.wait1()
    w_k.start1()
    rows_g.start2()
    w_q.start2()
    cuts = chain.step(lambda o, w: both(cut_rows, o, 1) + both(cut_rows, w, n_down), w_out, w_down)
    w_o, d0, d1 = (piece(*h) for h in cuts)
    w_k.wait1()
    w_q.wait2()
    w_v.start1()
    w_k.start2()
    cuts = chain.step(lambda g: both(cut_gate_up, g, n_gu), w_gate_up)
    g0, g1, g2, g3 = gus = [piece(*h) for h in cuts]
    w_v.wait1()
    w_k.wait2()
    w_o.start1()
    w_v.start2()
    normed_first = rows_a.wait()
    query_raw = chain.step(product, normed_first, w_q.pair)
    key_raw = chain.step(product, normed_first, w_k.pair)
    w_o.wait1()
    w_v.wait2()
    d0.start1()
    w_o.start2()
    value_raw = chain.step(product, normed_first, w_v.pair)
    saved = chain.step(lambda *a: attend(*a), *table, query_raw, key_raw, value_raw)
    attn_flat = saved[0]
    w_o.wait2()
    mixed = chain.step(lambda y, p: back([y], [p], bf16), attn_flat, w_o.pair)
    d0.wait1()
    d1.start1()
    mixed_out = RowSum(wires, chain, mixed)
    d0.start2()
    grad_half = rows_g.wait()
    d1.wait1()
    d0.wait2()
    g0.start1()
    d1.start2()
    act_0 = chain.step(product, grad_half, d0.pair)
    g0.wait1()
    d1.wait2()
    g1.start1()
    g0.start2()
    act_1 = chain.step(product, grad_half, d1.pair)
    grad_acts = [act_0, act_1]
    middle, scale_second, v = chain.step(rows.open_second, input_f, mixed_out.wait(), gains)
    g1.wait1()
    g0.wait2()
    g2.start1()
    rows_n = RowGather(wires, chain, v)
    g1.start2()
    g2.wait1()
    g1.wait2()
    g3.start1()
    g2.start2()
    g3.wait1()
    g2.wait2()
    g3.start2()
    normed_second = rows_n.wait()
    forward_gu(0)
    grads[0].odd()
    grads[0].start1()
    forward_gu(1)
    forward_gu(2)
    second = chain.step(lambda y, p: back(y, p, f32, turn=False), grads_gu, [g.pair for g in gus[:3]])
    g3.wait2()
    forward_gu(3)
    second = chain.step(lambda y, p, s: back([y], [p], bf16, s), grads_gu[3], g3.pair, second)
    grads[0].wait1()
    sum_second = RowSum(wires, chain, second)
    grads[1].odd()
    grads[1].start1()
    grads[0].even()
    grads[0].add()
    grads[1].even()
    grads[2].odd()
    acts = [jnp.concatenate(acts[k * per : (k + 1) * per], axis=1) for k in range(n_down)]
    grads += [Grad(wires, chain, sides, grad_half, a) for a in acts]
    grads[1].wait1()
    grads[2].start1()
    grads[0].start2()
    grads[1].add()
    grads[2].even()
    grads[3].odd()
    mlp_part = chain.step(lambda y, p: back(y, p, bf16), acts, [d0.pair, d1.pair])
    part_gain_mlp, grad_middle, v = chain.step(
        rows.close_second, sum_second.wait(), gains, middle, scale_second, grad_rows
    )
    grads[2].wait1()
    grads[0].wait2()
    rows_m = PairGather(wires, chain, sides, v)
    grads[3].start1()
    grads[1].start2()
    grads[2].add()
    grads[3].even()
    grads[4].odd()
    grads[3].wait1()
    grads[1].wait2()
    rows_m.wait1()
    rows_m.start2()
    grads[4].start1()
    grads[2].start2()
    grads[3].add()
    grads[4].even()
    grads[5].odd()
    grads[4].wait1()
    grads[2].wait2()
    grads[5].start1()
    grads[3].start2()
    mlp = RowSum(wires, chain, mlp_part)
    grads[4].add()
    grads[5].even()
    middle_half = rows_m.wait()
    grads.append(Grad(wires, chain, sides, middle_half, attn_flat))
    grads[6].odd()
    grad_mixed = chain.step(lambda x, p: product(x, p, bf16), middle_half, w_o.pair)
    grad_proj = chain.step(lambda *a: attend_back(*a), *table, saved, grad_mixed)
    grads += [Grad(wires, chain, sides, normed_first, g) for g in grad_proj]
    grads[5].wait1()
    grads[3].wait2()
    grads[6].start1()
    grads[4].start2()
    grads[5].add()
    grads[7].odd()
    first, part_gain_attn = chain.step(
        lambda y, p, x: back(y, p, bf16, normed=x), grad_proj, [w_q.pair, w_k.pair, w_v.pair], normed_first
    )
    grads[6].wait1()
    grads[4].wait2()
    sum_first = RowSum(wires, chain, first)
    grads[7].start1()
    grads[5].start2()
    grads[6].even()
    grads[6].add()
    grads[8].odd()
    grads[7].even()

    def open_gains(attn, mlp, gains):
        parts = jnp.concatenate([attn / gains[0:1].astype(f32), mlp]).reshape(2, dp, kb)
        return parts

    class GainSum:
        def __init__(self, total):
            self.total = total

        def start(self, bit):
            rows = self.total.shape[1] // 2
            if bit == PAIR:
                mine = jnp.where(side == 0, self.total[:, :1], self.total[:, 1:])
                send = jnp.where(side == 0, self.total[:, 1:], self.total[:, :1])
            else:
                mine, send = self.total[:, :rows], self.total[:, rows:]
            self.total = mine
            self.got = wires.over_dp(*chain.pin(send), bit)

        def start_tensor(self, mask):
            self.got = wires.over_tensor(*chain.pin(self.total), mask)

        def wait(self):
            self.total = self.total + chain.wait(self.got)

    gain_sum = GainSum(chain.step(open_gains, part_gain_attn, part_gain_mlp, gains))
    gain_sum.start(NEAR)

    def lay(which, shape, axis, place):
        block = tuple(n // 2 if a == axis else n for a, n in enumerate(shape))
        return chain.step(
            lambda t: laid_out(sides, t, shape, block, axis, place), [grads[i].terms for i in which]
        )

    def place_gu(ref, parts):
        for k, p in enumerate(parts):
            ref[:, 0, k * cg : (k + 1) * cg] = p[:, :cg]
            ref[:, 1, k * cg : (k + 1) * cg] = p[:, cg:]

    def place_rows(ref, parts):
        n = parts[0].shape[1]
        for k, p in enumerate(parts):
            ref[k * n : (k + 1) * n] = p.T

    def place_stack(ref, parts):
        for k, p in enumerate(parts):
            ref[k] = p

    grads[7].wait1()
    grads[5].wait2()
    grads[8].start1()
    grads[6].start2()
    grads[7].add()
    grads[8].even()
    grads[9].odd()
    grads[9].even()
    layer_out = chain.step(rows.close_layer, mlp.wait(), middle)
    gain_sum.wait()
    for bit in wires.far[:0:-1]:
        gain_sum.start(bit)
        gain_sum.wait()
    gain_sum.start(wires.far[0])
    grads[8].wait1()
    grads[6].wait2()
    grads[9].start1()
    grads[7].start2()
    grads[8].add()
    grad_gate_up = lay((0, 1, 2, 3), (kb, 2, 2 * ff), 2, place_gu)
    gain_sum.wait()
    gain_sum.start(PAIR)
    grad_down = lay((4, 5), (2 * ff, kb), 0, place_rows)
    grads[7].wait2()
    grads[8].start2()
    grads[9].wait1()
    grads[9].add()
    grads[8].wait_pair()
    grads[9].start2()
    grad_out = lay((6,), (2 * cols, kb), 0, place_rows)
    gain_sum.wait()
    gain_sum.start_tensor(1)
    grad_in = chain.step(rows.close_first, sum_first.wait(), gains, input_f, scale_first, grad_middle)
    gain_sum.wait()
    gain_sum.start_tensor(2)
    grads[8].wait2()
    gain_sum.wait()
    total = gain_sum.total[:, 0]
    grads[9].wait2()
    grad_qkv = lay((7, 8, 9), (3, kb, 2 * cols), 2, place_stack)
    return (layer_out, grad_in, total[0], grad_qkv, grad_out, total[1], grad_gate_up, grad_down)


def solution(mesh):
    placed = (
        P(("dp", "tensor"), None),
        P(("dp", "tensor"), None),
        P("dp"),
        P("dp"),
        P(None, "dp", "tensor"),
        P("tensor", "dp"),
        P("dp"),
        P("dp", None, "tensor"),
        P("tensor", "dp"),
    )
    dp, tp = mesh.shape["dp"], mesh.shape["tensor"]

    def body(*args):
        return on_device(dp, tp, *args)

    return jax.shard_map(
        body,
        mesh=mesh,
        in_specs=placed,
        out_specs=(
            P(("dp", "tensor"), None),
            P(("dp", "tensor"), None),
            P("dp"),
            P(None, "dp", "tensor"),
            P("tensor", "dp"),
            P("dp"),
            P("dp", None, "tensor"),
            P("tensor", "dp"),
        ),
        check_vma=False,
    )
```

```python
import math

import jax
import jax.numpy as jnp
from jax import lax
from jax.experimental import pallas as pl
from jax.experimental.pallas import tpu as pltpu
from jax.sharding import PartitionSpec as P

HEAD_DIM = 96
NORM_EPS = 1e-05
ROPE_BASE = 10000.0
AXES = ("dp", "tensor")
PAIR = 2
NEAR = 1
NEGATIVE = -1e30

bf16 = jnp.bfloat16
f32 = jnp.float32


def dot_last(a, b):
    return lax.dot_general(a, b, (((1,), (1,)), ((), ())), preferred_element_type=f32)


def dot_first(a, b):
    return lax.dot_general(a, b, (((0,), (0,)), ((), ())), preferred_element_type=f32)


def turned(u, low):
    width = u.shape[1]
    half = HEAD_DIM // 2
    return jnp.where(low, pltpu.roll(u, width - half, 1), pltpu.roll(u, half, 1))


def low_lanes(shape):
    lane = lax.broadcasted_iota(jnp.int32, shape, 1)
    low = lane < 0
    for h in range(shape[1] // HEAD_DIM):
        low = low | ((lane >= h * HEAD_DIM) & (lane < h * HEAD_DIM + HEAD_DIM // 2))
    return low


def group_block(ref):
    return ref[...]


def put_block(ref, v):
    ref[...] = v


def masked_scores(qh, kh, allowed):
    return jnp.where(allowed, dot_last(qh, kh) * (1.0 / math.sqrt(HEAD_DIM)), NEGATIVE)


def allowed_pairs(rows_ref, cols_ref, length):
    rp, cp = rows_ref[...], cols_ref[...]
    return (cp <= rp) & ((rp < length) == (cp < length))


def attend_kernel(len_ref, rows_ref, cols_ref, cos_ref, sin_ref, q_ref, k_ref, v_ref,
                  o_ref, qo_ref, ko_ref, vo_ref, lse_ref):
    allowed = allowed_pairs(rows_ref, cols_ref, len_ref[pl.program_id(0)])
    q, k = group_block(q_ref), group_block(k_ref)
    cosine, sine = (jnp.concatenate([r[...]] * (q.shape[1] // HEAD_DIM), axis=1) for r in (cos_ref, sin_ref))
    low = low_lanes(cosine.shape)
    q = q * cosine + turned(q, low) * sine
    k = k * cosine + turned(k, low) * sine
    v = group_block(v_ref)
    put_block(qo_ref, q.astype(bf16))
    put_block(ko_ref, k.astype(bf16))
    put_block(vo_ref, v.astype(bf16))
    outs, totals = [], []
    for h in range(q.shape[1] // HEAD_DIM):
        c = slice(h * HEAD_DIM, (h + 1) * HEAD_DIM)
        s = masked_scores(q[:, c].astype(bf16), k[:, c].astype(bf16), allowed)
        top = jnp.max(s, axis=1, keepdims=True)
        e = jnp.exp(s - top)
        total = jnp.sum(e, axis=1, keepdims=True)
        prob = (e * (1.0 / total)).astype(bf16)
        outs.append(jnp.dot(prob, v[:, c].astype(bf16), preferred_element_type=f32))
        totals.append(top + jnp.log(total))
    put_block(o_ref, jnp.concatenate(outs, axis=1).astype(bf16))
    put_block(lse_ref, jnp.concatenate(totals, axis=1))


def attend_back_kernel(len_ref, rows_ref, cols_ref, cos_ref, sin_ref, q_ref, k_ref, v_ref, o_ref, g_ref, lse_ref,
                       dq_ref, dk_ref, dv_ref):
    allowed = allowed_pairs(rows_ref, cols_ref, len_ref[pl.program_id(0)])
    q, k, v, g = (group_block(r).astype(f32) for r in (q_ref, k_ref, v_ref, g_ref))
    go = g * group_block(o_ref).astype(f32)
    totals = group_block(lse_ref)
    dqs, dks, dvs = [], [], []
    for h in range(q.shape[1] // HEAD_DIM):
        c = slice(h * HEAD_DIM, (h + 1) * HEAD_DIM)
        qh, kh, vh, gh = (u[:, c].astype(bf16) for u in (q, k, v, g))
        delta = jnp.sum(go[:, c], axis=1, keepdims=True)
        prob = jnp.exp(masked_scores(qh, kh, allowed) - totals[:, h : h + 1])
        ds = (prob * (dot_last(gh, vh) - delta) * (1.0 / math.sqrt(HEAD_DIM))).astype(bf16)
        dqs.append(jnp.dot(ds, kh, preferred_element_type=f32))
        dks.append(dot_first(ds, qh))
        dvs.append(dot_first(prob.astype(bf16), gh))
    cosine, sine = (jnp.concatenate([r[...]] * (q.shape[1] // HEAD_DIM), axis=1) for r in (cos_ref, sin_ref))
    low = low_lanes(cosine.shape)
    for ref, parts in ((dq_ref, dqs), (dk_ref, dks)):
        u = jnp.concatenate(parts, axis=1)
        put_block(ref, (u * cosine - turned(u, low) * sine).astype(bf16))
    put_block(dv_ref, jnp.concatenate(dvs, axis=1).astype(bf16))


def attend_specs(group_rows, cols, lanes):
    tall = pl.BlockSpec((group_rows, cols), lambda g: (g, 0))
    table = pl.BlockSpec((group_rows, HEAD_DIM), lambda g: (g, 0))
    head = [
        pl.BlockSpec(memory_space=pltpu.SMEM),
        pl.BlockSpec((group_rows, 1), lambda g: (g, 0)),
        pl.BlockSpec((1, group_rows), lambda g: (0, g)),
        table,
        table,
    ]
    return head, tall, pl.BlockSpec((group_rows, lanes), lambda g: (g, 0))


def attend(lengths, positions, cosine, sine, q, k, v):
    rows, cols = q.shape
    lanes = cols // HEAD_DIM
    head, tall, thin = attend_specs(rows // 2, cols, lanes)
    return run(
        attend_kernel, "attend", [((rows, cols), bf16)] * 4 + [((rows, lanes), f32)],
        [lengths, positions[:, None], positions[None, :], cosine, sine, q, k, v], (2,),
        head + [tall] * 3, [tall] * 4 + [thin],
    )


def attend_back(lengths, positions, cosine, sine, saved, g):
    o, q, k, v, lse = saved
    rows, cols = q.shape
    head, tall, thin = attend_specs(rows // 2, cols, cols // HEAD_DIM)
    return run(
        attend_back_kernel, "attend_back", [((rows, cols), bf16)] * 3,
        [lengths, positions[:, None], positions[None, :], cosine, sine, q, k, v, o, g, lse], (2,),
        head + [tall] * 5 + [thin], [tall] * 3,
    )


def run(kernel, name, outs, args, grid=(), in_specs=None, out_specs=None, scratch=(), scalars=0):
    whole = pl.BlockSpec(memory_space=pltpu.VMEM)
    if in_specs is None:
        in_specs = [whole] * (len(args) - scalars)
    if out_specs is None:
        out_specs = [whole] * len(outs)
    got = pl.pallas_call(
        kernel,
        out_shape=[jax.ShapeDtypeStruct(s, t) for s, t in outs],
        grid_spec=pltpu.PrefetchScalarGridSpec(
            num_scalar_prefetch=scalars, grid=grid, in_specs=in_specs, out_specs=out_specs, scratch_shapes=scratch
        ),
        compiler_params=pltpu.CompilerParams(vmem_limit_bytes=52 << 20),
        cost_estimate=pl.CostEstimate(flops=1, bytes_accessed=1, transcendentals=0),
        name=name,
    )(*args)
    return list(got)


SMALL = pl.BlockSpec(memory_space=pltpu.SMEM)
VMEM = pl.BlockSpec(memory_space=pltpu.VMEM)


def tiles(rows, width):
    return pl.BlockSpec((rows, width), lambda i: (i, 0))


def still(shape):
    return pl.BlockSpec(shape, lambda i: (0,) * len(shape), pipeline_mode=pl.Buffered(1))


def product(x, pair, dtype=f32):
    rows, width = x.shape
    k, n = pair[0].shape
    tile = rows // 4

    def kernel(x_ref, even, odd, out):
        total = jnp.dot(x_ref[:, :k], even[...], preferred_element_type=f32)
        total += jnp.dot(x_ref[:, k:], odd[...], preferred_element_type=f32)
        out[...] = total.astype(dtype)

    return run(
        kernel, "product", [((rows, n), dtype)], [x, *pair], (4,),
        [tiles(tile, width)] + [still((k, n))] * 2, [tiles(tile, n)],
    )[0]


def gated(x, pair, grad_act, column):
    rows, width = x.shape
    k, n = pair[0].shape
    c = n // 2
    tile = rows // 4

    def kernel(x_ref, even, odd, ga_ref, act, grad):
        total = jnp.dot(x_ref[:, :k], even[...], preferred_element_type=f32)
        total += jnp.dot(x_ref[:, k:], odd[...], preferred_element_type=f32)
        gate, up, ga = total[:, :c], total[:, c:], ga_ref[...]
        sig = jax.nn.sigmoid(gate)
        act[...] = (gate * sig * up).astype(bf16)
        grad[:, :c] = (ga * up * sig * (1.0 + gate * (1.0 - sig))).astype(bf16)
        grad[:, c:] = (ga * gate * sig).astype(bf16)

    return run(
        kernel, "gated", [((rows, c), bf16), ((rows, n), bf16)], [x, *pair, grad_act], (4,),
        [tiles(tile, width)] + [still((k, n))] * 2 + [pl.BlockSpec((tile, c), lambda i: (i, column))],
        [tiles(tile, c), tiles(tile, n)],
    )


def back(ys, pairs, dtype, part=None, turn=True, normed=None):
    rows = ys[0].shape[0]
    k = pairs[0][0].shape[0]
    count = len(ys)
    tile = rows // 4
    extra = [a for a in (part, normed) if a is not None]
    more = len(extra)

    def kernel(*refs):
        y_refs, w_refs, out = refs[:count], refs[count : 3 * count], refs[3 * count + more]
        for s in range(2):
            c = slice(s * k, (s + 1) * k)
            total = refs[3 * count][:, c] if part is not None else None
            for y, w in zip(y_refs, w_refs[s::2]):
                term = dot_last(y[...], w[...])
                total = term if total is None else total + term
            if normed is not None:
                sums = jnp.sum(total * refs[3 * count][:, c].astype(f32), axis=0, keepdims=True)

                @pl.when(pl.program_id(0) == 0)
                def _():
                    refs[-1][:, c] = sums

                @pl.when(pl.program_id(0) > 0)
                def _():
                    refs[-1][:, c] += sums

            total = total.astype(dtype)
            if not turn:
                out[:, c] = total
                continue

            i = pl.program_id(0)
            swapped = (i == 1) | (i == 2)

            @pl.when(jnp.logical_not(swapped))
            def _():
                out[:, c] = total

            @pl.when(swapped)
            def _():
                out[: tile // 2, c] = total[tile // 2 :]
                out[tile // 2 :, c] = total[: tile // 2]

    flat = [w for p in pairs for w in p]
    outs = [((rows, 2 * k), dtype)] + ([] if normed is None else [((1, 2 * k), f32)])
    got = run(
        kernel, "back", outs, [*ys, *flat, *extra], (4,),
        [tiles(tile, y.shape[1]) for y in ys] + [still(w.shape) for w in flat] + [tiles(tile, 2 * k)] * more,
        [
            pl.BlockSpec((tile, 2 * k), lambda i: (jnp.where(i < 2, i, 5 - i) if turn else i, 0)),
            pl.BlockSpec((1, 2 * k), lambda i: (0, 0)),
        ][: len(outs)],
    )
    return got[0] if normed is None else got


def side_by_side(side, mine, theirs):
    rows, n = mine.shape

    def kernel(side_ref, a, b, out):
        for q, ref in enumerate((a, b)):

            @pl.when(pl.program_id(0) == q)
            def _(ref=ref):
                out[...] = ref[...].reshape(1, rows, n)

    whole = pl.BlockSpec((rows, n), lambda i, s: (0, 0))
    return run(
        kernel, "side_by_side", [((2, rows, n), bf16)], [side, mine, theirs], (2,), [whole] * 2,
        [pl.BlockSpec((1, rows, n), lambda i, s: (i ^ s[0], 0, 0))], scalars=1,
    )[0]


def weight_part(x, y, first, count, dtype):
    rows = x.shape[0]
    n = y.shape[1]
    tile = count if count <= 768 else count // 2
    base = first // tile

    def kernel(x_ref, y_ref, out):
        out[...] = dot_first(x_ref[...], y_ref[...]).astype(dtype)

    return run(
        kernel, "weight_part", [((count, n), dtype)], [x, y], (count // tile,),
        [pl.BlockSpec((rows, tile), lambda i: (0, i + base)), still(y.shape)], [tiles(tile, n)],
    )[0]


class Rows:
    def __init__(self, wires, info, rows, width):
        self.wires, self.info, self.rows, self.width = wires, info, rows, width
        self.kb = width // wires.dp
        self.inside = self.kb % 128 == 0

    def load_relative(self, ref, info):
        if not self.inside:
            return ref[...].astype(f32)
        kb = self.kb
        parts = []
        for m in self.wires.order:
            parts.append(ref[:, pl.ds(pl.multiple_of((info[0] ^ m) * kb, 128), kb)].astype(f32))
        return jnp.concatenate(parts, axis=1)

    def store_absolute(self, ref, value, scratch, info):
        if not self.inside:
            ref[...] = value
            return
        kb, half = self.kb, self.wires.dp // 2
        scratch[...] = value
        for j in range(self.wires.dp):
            m = info[0] ^ j
            place = (m >> 1) + half * (m & 1)
            ref[:, j * kb : (j + 1) * kb] = scratch[:, pl.ds(pl.multiple_of(place * kb, 128), kb)]

    def relative(self, x):
        return x if self.inside else self.wires.to_relative(x, self.info[0])

    def absolute(self, x):
        return x if self.inside else self.wires.to_absolute(x, self.info[0])

    def live(self, info, shape):
        row = info[1] * shape[0] + lax.broadcasted_iota(jnp.int32, (shape[0], 1), 0)
        return (row < info[2]).astype(f32)

    def outs(self, *dtypes):
        return [((self.rows, self.width), t) for t in dtypes]

    def open_first(self, x, gains):
        def kernel(info, x_ref, gain_ref, rel, scale_ref, v):
            x = self.load_relative(x_ref, info)
            scale = lax.rsqrt(jnp.mean(x * x, axis=1, keepdims=True) + NORM_EPS)
            rel[...] = x
            scale_ref[...] = scale
            v[...] = (x * scale * gain_ref[0:1].astype(f32)).astype(bf16)

        return run(
            kernel, "open_first", self.outs(f32) + [((self.rows, 1), f32)] + self.outs(bf16),
            [self.info, self.relative(x), gains], in_specs=[SMALL, VMEM, VMEM],
        )

    def open_cotangent(self, c):
        def kernel(info, c_ref, g, v):
            x = self.load_relative(c_ref, info)
            x = x * self.live(info, x.shape)
            g[...] = x
            v[...] = x.astype(bf16)

        return run(
            kernel, "open_cotangent", self.outs(f32, bf16), [self.info, self.relative(c)], in_specs=[SMALL, VMEM]
        )

    def open_second(self, x, got, gains):
        def kernel(x_ref, got_ref, gain_ref, mid, scale_ref, v):
            middle = x_ref[...] + got_ref[...].astype(f32)
            scale = lax.rsqrt(jnp.mean(middle * middle, axis=1, keepdims=True) + NORM_EPS)
            mid[...] = middle
            scale_ref[...] = scale
            v[...] = (middle * scale * gain_ref[1:2].astype(f32)).astype(bf16)

        return run(
            kernel, "open_second", self.outs(f32) + [((self.rows, 1), f32)] + self.outs(bf16), [x, got, gains]
        )

    def norm_back(self, got_ref, gain, x_ref, scale_ref, rows_ref, part=None):
        grad = got_ref[...].astype(f32)
        scale = scale_ref[...]
        unit = x_ref[...] * scale
        if part is not None:
            part[...] = jnp.sum(grad * unit, axis=0, keepdims=True)
        e = grad * gain
        return rows_ref[...] + scale * (e - unit * jnp.mean(e * unit, axis=1, keepdims=True))

    def close_second(self, got, gains, middle, scale, rows):
        def kernel(got_ref, gain_ref, x_ref, scale_ref, rows_ref, part, mid, v):
            grad = self.norm_back(got_ref, gain_ref[1:2].astype(f32), x_ref, scale_ref, rows_ref, part)
            mid[...] = grad
            v[...] = grad.astype(bf16)

        return run(
            kernel, "close_second", [((1, self.width), f32)] + self.outs(f32, bf16),
            [got, gains, middle, scale, rows],
        )

    def close_first(self, got, gains, x, scale, rows):
        def kernel(info, got_ref, gain_ref, x_ref, scale_ref, rows_ref, out, scratch):
            grad = self.norm_back(got_ref, gain_ref[0:1].astype(f32), x_ref, scale_ref, rows_ref)
            self.store_absolute(out, grad, scratch, info)

        out, = run(
            kernel, "close_first", self.outs(f32),
            [self.info, got, gains, x, scale, rows], in_specs=[SMALL] + [VMEM] * 5,
            scratch=[pltpu.VMEM((self.rows, self.width), f32)],
        )
        return self.absolute(out)

    def close_layer(self, got, middle):
        def kernel(info, got_ref, mid_ref, out, scratch):
            total = mid_ref[...] + got_ref[...].astype(f32)
            self.store_absolute(out, total * self.live(info, total.shape), scratch, info)

        out, = run(
            kernel, "close_layer", self.outs(f32), [self.info, got, middle], in_specs=[SMALL] + [VMEM] * 2,
            scratch=[pltpu.VMEM((self.rows, self.width), f32)],
        )
        return self.absolute(out)


def in_order(side, own, far, far_pair, pair):
    kb, n = own.shape

    def kernel(side_ref, *refs):
        i, s = pl.program_id(0), side_ref[0]
        for at, ref in enumerate((refs[0], refs[3], refs[1], refs[2])):

            @pl.when((i ^ s) == at)
            def _(ref=ref):
                refs[-1][...] = ref[...]

    whole = pl.BlockSpec((kb, n), lambda i, s: (0, 0))
    return run(
        kernel, "in_order", [((4 * kb, n), bf16)], [side, own, far, far_pair, pair], (4,), [whole] * 4,
        [pl.BlockSpec((kb, n), lambda i, s: (i, 0))], scalars=1,
    )[0]


def added(side, keep, got, at, kb, dtypes):
    n = keep.shape[1]

    def kernel(side_ref, k0, g0, k1, g1, first, second):
        first[...] = (k0[...] + g0[...].astype(f32)).astype(first.dtype)
        second[...] = (k1[...] + g1[...].astype(f32)).astype(second.dtype)

    block = lambda q: pl.BlockSpec((kb, n), lambda i, s: (at + (q ^ s[0]), 0))
    whole = pl.BlockSpec((kb, n), lambda i, s: (0, 0))
    return run(
        kernel, "added", [((kb, n), t) for t in dtypes], [side, keep, got, keep, got], (1,),
        [block(0), block(0), block(1), block(1)], [whole, whole], scalars=1,
    )


def cut_gate_up(side, w, count):
    kb, _, width = w.shape
    c = width // 2 // count

    def kernel(side_ref, w_ref, *outs):
        for k, out in enumerate(outs):
            out[:, :c] = w_ref[:, 0, k * c : (k + 1) * c]
            out[:, c:] = w_ref[:, 1, k * c : (k + 1) * c]

    return run(
        kernel, "cut_gate_up", [((kb, 2 * c), bf16)] * count, [side, w], (1,),
        [pl.BlockSpec((kb, 2, width // 2), lambda i, s: (0, 0, s[0]))],
        [pl.BlockSpec((kb, 2 * c), lambda i, s: (0, 0))] * count, scalars=1,
    )


def cut_rows(side, w, count):
    rows, kb = w.shape
    c = rows // 2 // count

    def kernel(side_ref, w_ref, *outs):
        for k, out in enumerate(outs):
            out[...] = w_ref[k * c : (k + 1) * c].T

    return run(
        kernel, "cut_rows", [((kb, c), bf16)] * count, [side, w], (1,),
        [pl.BlockSpec((rows // 2, kb), lambda i, s: (s[0], 0))],
        [pl.BlockSpec((kb, c), lambda i, s: (0, 0))] * count, scalars=1,
    )


def cut_columns(side, w):
    count, kb, width = w.shape

    def kernel(side_ref, w_ref, *outs):
        for k, out in enumerate(outs):
            out[...] = w_ref[k]

    return run(
        kernel, "cut_columns", [((kb, width // 2), bf16)] * count, [side, w], (1,),
        [pl.BlockSpec((count, kb, width // 2), lambda i, s: (0, 0, s[0]))],
        [pl.BlockSpec((kb, width // 2), lambda i, s: (0, 0))] * count, scalars=1,
    )


def laid_out(side, terms, shape, block, axis, place):
    count = len(terms)

    def kernel(side_ref, *refs):
        out = refs[-1]

        @pl.when(pl.program_id(0) == 0)
        def _():
            place(out, [refs[4 * q][...] + refs[4 * q + 1][...].astype(f32) for q in range(count)])

        @pl.when(pl.program_id(0) == 1)
        def _():
            place(
                out, [refs[4 * q + 2][...].astype(f32) + refs[4 * q + 3][...].astype(f32) for q in range(count)]
            )

    def index(w, side_ref):
        at = w ^ side_ref[0]
        return tuple(at if a == axis else 0 for a in range(len(shape)))

    arrays = [a for t in terms for a in t]
    return run(
        kernel, "laid_out", [(shape, f32)], [side, *arrays], (2,),
        [pl.BlockSpec(a.shape, lambda w, s: (0, 0)) for a in arrays], [pl.BlockSpec(block, index)], scalars=1,
    )[0]


class Wires:
    def __init__(self, dp, tp):
        self.dp, self.tp = dp, tp
        self.order = list(range(0, dp, 2)) + list(range(1, dp, 2))
        self.far = []
        bit = 2 * PAIR
        while bit < dp:
            self.far.append(bit)
            bit *= 2

    def over_dp(self, value, mask):
        pairs = []
        for d in range(self.dp):
            for t in range(self.tp):
                pairs.append((d * self.tp + t, (d ^ mask) * self.tp + t))
        return lax.ppermute(value, AXES, pairs)

    def over_tensor(self, value, mask):
        pairs = []
        for d in range(self.dp):
            for t in range(self.tp):
                pairs.append((d * self.tp + t, d * self.tp + (t ^ mask)))
        return lax.ppermute(value, AXES, pairs)

    def to_relative(self, value, d):
        width = value.shape[1] // self.dp
        return jnp.concatenate(
            [lax.dynamic_slice_in_dim(value, (d ^ m) * width, width, 1) for m in self.order], axis=1
        )

    def to_absolute(self, value, d):
        width = value.shape[1] // self.dp
        parts = []
        for j in range(self.dp):
            m = d ^ j
            place = (m >> 1) + (self.dp // 2) * (m & 1)
            parts.append(lax.dynamic_slice_in_dim(value, place * width, width, 1))
        return jnp.concatenate(parts, axis=1)

    def walk(self):
        return [t ^ (t >> 1) for t in range(self.tp)]

    def pairs(self, walk):
        there = self.walk() if walk else list(range(self.tp))
        back = there[::-1] if walk else there
        return [
            [d * self.tp + t for t in there] + [(d ^ PAIR) * self.tp + t for t in back]
            for d in range(self.dp)
            if not d & PAIR
        ]

    def singles(self):
        return [[d * self.tp + t for t in range(self.tp)] for d in range(self.dp)]


def halves(value, side, axis):
    width = value.shape[axis] // 2
    own = lax.dynamic_slice_in_dim(value, side * width, width, axis)
    other = lax.dynamic_slice_in_dim(value, (1 - side) * width, width, axis)
    return own, other


def joined(own, other, side, axis):
    low = jnp.where(side == 0, own, other)
    high = jnp.where(side == 0, other, own)
    return jnp.concatenate([low, high], axis=axis)


class Chain:
    def __init__(self):
        self.last = ()

    def pin(self, *values):
        return lax.optimization_barrier((values, self.last))[0]

    def wait(self, *values):
        self.last = self.pin(*values)
        return self.last if len(values) > 1 else self.last[0]

    def step(self, function, *values):
        out = function(*self.pin(*values))
        self.last = out
        return out


class Piece:
    def __init__(self, wires, chain, side, own, other):
        self.wires, self.chain, self.side, self.own, self.other = wires, chain, side, own, other

    def start1(self):
        own, other = self.chain.pin(self.own, self.other)
        far = self.wires.far[0]
        self.got = [
            self.wires.over_dp(own, far), self.wires.over_dp(other, far ^ PAIR), self.wires.over_dp(other, PAIR)
        ]

    def wait1(self):
        self.got = self.chain.wait(*self.got)

    def start2(self):
        blocks = self.chain.step(in_order, self.side, self.own, *self.got)
        for bit in self.wires.far[1:]:
            blocks = jnp.concatenate([blocks, self.chain.wait(self.wires.over_dp(blocks, bit))], axis=0)
        self.blocks = blocks
        self.got = self.wires.over_dp(*self.chain.pin(blocks), NEAR)

    def wait2(self):
        self.pair = (self.blocks, self.chain.wait(self.got))


class Grad:
    def __init__(self, wires, chain, side, x, y):
        self.wires, self.chain, self.side, self.x, self.y = wires, chain, side, x, y
        self.k = x.shape[1] // 2

    def odd(self):
        self.send = self.chain.step(lambda x, y: weight_part(x, y, self.k, self.k, bf16), self.x, self.y)

    def start1(self):
        self.got = self.wires.over_dp(*self.chain.pin(self.send), NEAR)

    def wait1(self):
        self.near = self.chain.wait(self.got)

    def even(self):
        self.ahead = self.chain.step(lambda x, y: weight_part(x, y, 0, self.k, f32), self.x, self.y)

    def add(self):
        wires, chain = self.wires, self.chain
        kb = 2 * self.k // wires.dp
        if not wires.far[1:]:
            self.sends = chain.step(
                lambda s, e, g: added(s, e, g, 2, kb, (bf16, bf16)), self.side, self.ahead, self.near
            )
            self.keep, pair = chain.step(
                lambda s, e, g: added(s, e, g, 0, kb, (f32, bf16)), self.side, self.ahead, self.near
            )
            self.sends = [*self.sends, pair]
            return
        total = self.ahead + self.near.astype(f32)
        for b in reversed(wires.far[1:]):
            rows = total.shape[0] // 2
            got = chain.wait(wires.over_dp(total[rows:].astype(bf16), b))
            total = total[:rows] + got.astype(f32)
        cut = lambda p: lax.dynamic_slice_in_dim(total, (p ^ self.side[0]) * kb, kb, 0)
        far = lambda p: lax.dynamic_slice_in_dim(total, (2 + (p ^ self.side[0])) * kb, kb, 0)
        self.keep = cut(0)
        self.sends = [far(0).astype(bf16), far(1).astype(bf16), cut(1).astype(bf16)]

    def start2(self):
        bit = self.wires.far[0]
        sends = self.chain.pin(*self.sends)
        self.got = [self.wires.over_dp(v, m) for v, m in zip(sends, (bit, bit ^ PAIR, PAIR))]

    def wait_pair(self):
        self.got[2] = self.chain.wait(self.got[2])

    def wait2(self):
        self.terms = [self.keep, *self.chain.wait(*self.got)]


class RowGather:
    def __init__(self, wires, chain, value):
        self.chain = chain
        self.got = lax.all_gather(
            *chain.pin(value), AXES, axis=0, tiled=True, axis_index_groups=wires.pairs(False)
        )

    def wait(self):
        return self.chain.wait(self.got)


class PairGather:
    def __init__(self, wires, chain, side, value):
        self.wires, self.chain, self.side, self.value = wires, chain, side, value
        self.got = wires.over_dp(*chain.pin(value), PAIR)

    def wait1(self):
        self.both = self.chain.step(side_by_side, self.side, self.value, self.chain.wait(self.got))

    def start2(self):
        got = lax.all_gather(
            *self.chain.pin(self.both), AXES, axis=1, tiled=True, axis_index_groups=self.wires.singles()
        )
        self.got = got.reshape(-1, got.shape[2])

    def wait(self):
        return self.chain.wait(self.got)


class RowSum:
    def __init__(self, wires, chain, value):
        self.chain = chain
        self.got = lax.psum_scatter(
            *chain.pin(value), AXES, scatter_dimension=0, tiled=True, axis_index_groups=wires.pairs(True)
        )

    def wait(self):
        return self.chain.wait(self.got)


def on_device(dp, tp, hidden_in, cotangent, lengths, gain_attn, w_qkv, w_out, gain_mlp, w_gate_up, w_down):
    wires = Wires(dp, tp)
    chain = Chain()
    d = lax.axis_index("dp").astype(jnp.int32)
    t = lax.axis_index("tensor").astype(jnp.int32)
    side = (d // PAIR) % 2
    local_rows, width = hidden_in.shape
    group_rows = local_rows * tp
    kb = width // dp
    cols = w_qkv.shape[2] // 2
    rows = Rows(wires, jnp.stack([d - PAIR * side, t, lengths[0]]), local_rows, width)

    sides = jnp.reshape(side, (1,))
    n_down, n_gu = 2, 4
    ff = w_down.shape[0] // 2
    cut, cg = ff // n_down, ff // n_gu

    def piece(own, other):
        return Piece(wires, chain, sides, own, other)

    def both(cut, w, *count):
        return list(zip(*(cut(s, w, *count) for s in (sides, 1 - sides))))

    per = n_gu // n_down
    acts, grads_gu, grads = [], [], []

    def forward_gu(k):
        act, g = chain.step(lambda *a: gated(*a, k % per), normed_second, gus[k].pair, grad_acts[k // per])
        acts.append(act)
        grads_gu.append(g)
        grads.append(Grad(wires, chain, sides, normed_second, g))

    positions = jnp.tile(jnp.arange(group_rows, dtype=jnp.int32), 2)
    exponent = jnp.arange(HEAD_DIM // 2).astype(f32) * (2.0 / HEAD_DIM)
    frequency = ROPE_BASE ** (-exponent)
    angles = positions.astype(f32)[:, None] * frequency[None, :]
    cosine = jnp.concatenate([jnp.cos(angles), jnp.cos(angles)], axis=1)
    sine = jnp.concatenate([-jnp.sin(angles), jnp.sin(angles)], axis=1)

    gains = jnp.stack([gain_attn, gain_mlp])[:, None]
    pair_length = wires.over_dp(lengths, PAIR)

    def ordered(mine, theirs, axis):
        return jnp.concatenate(
            [jnp.where(side == 0, mine, theirs), jnp.where(side == 0, theirs, mine)], axis=axis
        )

    masks = [PAIR, wires.far[0], wires.far[0] ^ PAIR]
    got = [wires.over_dp(gains, m) for m in masks]
    grad_rows, gv = chain.step(rows.open_cotangent, cotangent)
    got = chain.wait(*got)
    rows_g = PairGather(wires, chain, sides, gv)
    w_q, w_k, w_v = (piece(*h) for h in both(cut_columns, w_qkv))
    gains = jnp.concatenate([ordered(gains, got[0], 1), ordered(got[1], got[2], 1)], axis=1)
    for bit in wires.far[1:]:
        gains = jnp.concatenate([gains, chain.wait(wires.over_dp(*chain.pin(gains), bit))], axis=1)
    gains = jnp.concatenate([gains, chain.wait(wires.over_dp(*chain.pin(gains), NEAR))], axis=1)
    gains = gains.reshape(2, width)
    input_f, scale_first, v = chain.step(rows.open_first, hidden_in, gains)
    rows_g.wait1()
    rows_a = RowGather(wires, chain, v)
    w_q.start1()
    table = chain.step(
        lambda a, b, *c: (ordered(a, b, 0), *c), lengths, pair_length, positions, cosine, sine
    )
    w_q.wait1()
    w_k.start1()
    rows_g.start2()
    w_q.start2()
    cuts = chain.step(lambda o, w: both(cut_rows, o, 1) + both(cut_rows, w, n_down), w_out, w_down)
    w_o, d0, d1 = (piece(*h) for h in cuts)
    w_k.wait1()
    w_q.wait2()
    w_v.start1()
    w_k.start2()
    cuts = chain.step(lambda g: both(cut_gate_up, g, n_gu), w_gate_up)
    g0, g1, g2, g3 = gus = [piece(*h) for h in cuts]
    w_v.wait1()
    w_k.wait2()
    w_o.start1()
    w_v.start2()
    normed_first = rows_a.wait()
    query_raw = chain.step(product, normed_first, w_q.pair)
    key_raw = chain.step(product, normed_first, w_k.pair)
    w_o.wait1()
    w_v.wait2()
    d0.start1()
    w_o.start2()
    value_raw = chain.step(product, normed_first, w_v.pair)
    saved = chain.step(lambda *a: attend(*a), *table, query_raw, key_raw, value_raw)
    attn_flat = saved[0]
    w_o.wait2()
    mixed = chain.step(lambda y, p: back([y], [p], bf16), attn_flat, w_o.pair)
    d0.wait1()
    d1.start1()
    mixed_out = RowSum(wires, chain, mixed)
    d0.start2()
    grad_half = rows_g.wait()
    d1.wait1()
    d0.wait2()
    g0.start1()
    d1.start2()
    act_0 = chain.step(product, grad_half, d0.pair)
    g0.wait1()
    d1.wait2()
    g1.start1()
    g0.start2()
    act_1 = chain.step(product, grad_half, d1.pair)
    grad_acts = [act_0, act_1]
    middle, scale_second, v = chain.step(rows.open_second, input_f, mixed_out.wait(), gains)
    g1.wait1()
    g0.wait2()
    g2.start1()
    rows_n = RowGather(wires, chain, v)
    g1.start2()
    g2.wait1()
    g1.wait2()
    g3.start1()
    g2.start2()
    g3.wait1()
    g2.wait2()
    g3.start2()
    normed_second = rows_n.wait()
    forward_gu(0)
    grads[0].odd()
    grads[0].start1()
    forward_gu(1)
    forward_gu(2)
    second = chain.step(lambda y, p: back(y, p, f32, turn=False), grads_gu, [g.pair for g in gus[:3]])
    g3.wait2()
    forward_gu(3)
    second = chain.step(lambda y, p, s: back([y], [p], bf16, s), grads_gu[3], g3.pair, second)
    grads[0].wait1()
    sum_second = RowSum(wires, chain, second)
    grads[1].odd()
    grads[1].start1()
    grads[0].even()
    grads[0].add()
    grads[1].even()
    grads[2].odd()
    acts = [jnp.concatenate(acts[k * per : (k + 1) * per], axis=1) for k in range(n_down)]
    grads += [Grad(wires, chain, sides, grad_half, a) for a in acts]
    grads[1].wait1()
    grads[2].start1()
    grads[0].start2()
    grads[1].add()
    grads[2].even()
    grads[3].odd()
    part_gain_mlp, grad_middle, v = chain.step(
        rows.close_second, sum_second.wait(), gains, middle, scale_second, grad_rows
    )
    grads[2].wait1()
    grads[0].wait2()
    rows_m = PairGather(wires, chain, sides, v)
    grads[3].start1()
    grads[1].start2()
    grads[2].add()
    grads[3].even()
    grads[4].odd()
    mlp_part = chain.step(lambda y, p: back(y, p, bf16), acts, [d0.pair, d1.pair])
    grads[3].wait1()
    grads[1].wait2()
    rows_m.wait1()
    rows_m.start2()
    grads[4].start1()
    grads[2].start2()
    grads[3].add()
    grads[4].even()
    grads[5].odd()
    grads[5].even()
    grads[4].wait1()
    grads[2].wait2()
    grads[5].start1()
    grads[3].start2()
    mlp = RowSum(wires, chain, mlp_part)
    grads[4].add()
    middle_half = rows_m.wait()
    grads.append(Grad(wires, chain, sides, middle_half, attn_flat))
    grads[6].odd()
    grad_mixed = chain.step(lambda x, p: product(x, p, bf16), middle_half, w_o.pair)
    grad_proj = chain.step(lambda *a: attend_back(*a), *table, saved, grad_mixed)
    grads += [Grad(wires, chain, sides, normed_first, g) for g in grad_proj]
    grads[5].wait1()
    grads[3].wait2()
    grads[6].start1()
    grads[4].start2()
    grads[5].add()
    grads[7].odd()
    first, part_gain_attn = chain.step(
        lambda y, p, x: back(y, p, bf16, normed=x), grad_proj, [w_q.pair, w_k.pair, w_v.pair], normed_first
    )
    grads[6].wait1()
    grads[4].wait2()
    sum_first = RowSum(wires, chain, first)
    grads[7].start1()
    grads[5].start2()
    grads[6].even()
    grads[6].add()
    grads[8].odd()
    grads[7].even()

    def open_gains(attn, mlp, gains):
        parts = jnp.concatenate([attn / gains[0:1].astype(f32), mlp]).reshape(2, dp, kb)
        return parts

    class GainSum:
        def __init__(self, total):
            self.total = total

        def start(self, bit):
            rows = self.total.shape[1] // 2
            if bit == PAIR:
                mine = jnp.where(side == 0, self.total[:, :1], self.total[:, 1:])
                send = jnp.where(side == 0, self.total[:, 1:], self.total[:, :1])
            else:
                mine, send = self.total[:, :rows], self.total[:, rows:]
            self.total = mine
            self.got = wires.over_dp(*chain.pin(send), bit)

        def start_tensor(self, mask):
            self.got = wires.over_tensor(*chain.pin(self.total), mask)

        def wait(self):
            self.total = self.total + chain.wait(self.got)

    gain_sum = GainSum(chain.step(open_gains, part_gain_attn, part_gain_mlp, gains))
    gain_sum.start(NEAR)

    def lay(which, shape, axis, place):
        block = tuple(n // 2 if a == axis else n for a, n in enumerate(shape))
        return chain.step(
            lambda t: laid_out(sides, t, shape, block, axis, place), [grads[i].terms for i in which]
        )

    def place_gu(ref, parts):
        for k, p in enumerate(parts):
            ref[:, 0, k * cg : (k + 1) * cg] = p[:, :cg]
            ref[:, 1, k * cg : (k + 1) * cg] = p[:, cg:]

    def place_rows(ref, parts):
        n = parts[0].shape[1]
        for k, p in enumerate(parts):
            ref[k * n : (k + 1) * n] = p.T

    def place_stack(ref, parts):
        for k, p in enumerate(parts):
            ref[k] = p

    grads[7].wait1()
    grads[5].wait2()
    grads[8].start1()
    grads[6].start2()
    grads[7].add()
    grads[8].even()
    grads[9].odd()
    grads[9].even()
    layer_out = chain.step(rows.close_layer, mlp.wait(), middle)
    gain_sum.wait()
    for bit in wires.far[:0:-1]:
        gain_sum.start(bit)
        gain_sum.wait()
    gain_sum.start(wires.far[0])
    grads[8].wait1()
    grads[6].wait2()
    grads[9].start1()
    grads[7].start2()
    grads[8].add()
    grad_gate_up = lay((0, 1, 2, 3), (kb, 2, 2 * ff), 2, place_gu)
    gain_sum.wait()
    gain_sum.start(PAIR)
    grad_down = lay((4, 5), (2 * ff, kb), 0, place_rows)
    grads[7].wait2()
    grads[8].start2()
    grads[9].wait1()
    grads[9].add()
    grads[8].wait_pair()
    grads[9].start2()
    grad_out = lay((6,), (2 * cols, kb), 0, place_rows)
    gain_sum.wait()
    gain_sum.start_tensor(1)
    grad_in = chain.step(rows.close_first, sum_first.wait(), gains, input_f, scale_first, grad_middle)
    gain_sum.wait()
    gain_sum.start_tensor(2)
    grads[8].wait2()
    gain_sum.wait()
    total = gain_sum.total[:, 0]
    grads[9].wait2()
    grad_qkv = lay((7, 8, 9), (3, kb, 2 * cols), 2, place_stack)
    return (layer_out, grad_in, total[0], grad_qkv, grad_out, total[1], grad_gate_up, grad_down)


def solution(mesh):
    placed = (
        P(("dp", "tensor"), None),
        P(("dp", "tensor"), None),
        P("dp"),
        P("dp"),
        P(None, "dp", "tensor"),
        P("tensor", "dp"),
        P("dp"),
        P("dp", None, "tensor"),
        P("tensor", "dp"),
    )
    dp, tp = mesh.shape["dp"], mesh.shape["tensor"]

    def body(*args):
        return on_device(dp, tp, *args)

    return jax.shard_map(
        body,
        mesh=mesh,
        in_specs=placed,
        out_specs=(
            P(("dp", "tensor"), None),
            P(("dp", "tensor"), None),
            P("dp"),
            P(None, "dp", "tensor"),
            P("tensor", "dp"),
            P("dp"),
            P("dp", None, "tensor"),
            P("tensor", "dp"),
        ),
        check_vma=False,
    )
```
